32 devices in a mesh: groups: 2 (over y), seq: 4 (over z), rep: 2 (over x), sub: 2 (over core).
Axes of the slice: x: 2, y: 2, z: 4, core: 2. Of those that a mesh axis runs over, the one named last changes fastest.
Arguments:
- queries: bfloat16 [4, 512, 32, 384], P(('groups', 'rep'), 'seq', None, 'sub'), parts along dimension 0, may hold values from -64 to 64
- grad_out: bfloat16 [4, 512, 32, 256], P(('groups', 'rep'), 'seq', None, 'sub'), parts along dimension 0, may hold values from -6 to 6
- latent_kv: bfloat16 [4, 512, 576], P(('groups', 'rep'), 'seq'), parts along dimension 0, may hold values from -24 to 24
- key_up: bfloat16 [32, 2, 128, 512], P('seq', 'sub'), may hold values from -0.25 to 0.25
- value_up: bfloat16 [32, 2, 512, 128], P('seq', 'sub'), may hold values from -0.25 to 0.25
- key_blocks: int32 [4, 4, 3], P(('groups', 'rep')), parts along dimension 0, may hold values from 0 to 3, as said below
- block_counts: int32 [4, 4], P(('groups', 'rep')), parts along dimension 0, may hold values from 1 to 3, as said below
Outputs:
- grad_queries: bfloat16 [4, 512, 32, 384], P(('groups', 'rep'), 'seq', None, 'sub'), parts along dimension 0
- grad_latent: float32 [4, 512, 576], P(('groups', 'rep'), 'seq', 'sub'), parts along dimension 0
- grad_key_up: float32 [64, 2, 128, 512], P(('groups', 'seq'), 'sub', 'rep'), parts along dimension 0
- grad_value_up: float32 [64, 2, 512, 128], P(('groups', 'seq'), 'sub', 'rep'), parts along dimension 0
The draws below stay inside these ranges and needn't reach their ends.
There are 2 independent parts, one for each index of `groups`. The reference program is written for one: setup_inputs(seed, part) draws one part's arguments, and reference() takes and returns one part's arrays. A program takes and returns all parts, laid end to end along the dimension named above; an argument that names none is the same for every part. Nothing has to cross between parts.
Inputs may be any that keep to these rules, and one draw needn't show every extreme that they name: `key_blocks`: row b of a sequence lists key blocks for query block b: its first entry is b, its first block_counts[b] entries are distinct and none exceeds b, and the remaining entries equal b. `block_counts`: query block b lists at most min(b + 1, 3) key blocks; the last query block of each sequence lists exactly 3.
All inputs are finite; a program needn't handle non-finite values.
Results may differ from the reference program's by a relative error of at most 0.012.
Values may be sent and summed in bfloat16 or wider, within the bound.
A program may use at most 128 MiB of HBM per device.

```python
import math
import jax
import jax.numpy as jnp
from jax import lax

NOPE = 128
VD = 128
LAT = 512
BLK = 128
MAXB = 3
HP = 32
QD = 192
KVW = 576
SEQS = 2
L = 512
NQB = 4


def latent_draw(key):
    folded = jax.random.fold_in(key, 101)
    key_one = jax.random.fold_in(folded, 0)
    values = jnp.clip(jax.random.normal(key_one, (SEQS, L, KVW), jnp.float32), -6.0, 6.0)
    return values


def draw_latent_kv(key, part):
    return latent_draw(key).astype(jnp.bfloat16)


def draw_queries(key, part):
    folded = jax.random.fold_in(key, 202)
    key_one = jax.random.fold_in(folded, 0)
    values = jnp.clip(jax.random.normal(key_one, (SEQS, L, HP, 2 * QD), jnp.float32), -6.0, 6.0)
    return values.astype(jnp.bfloat16)


def block_lists(key):
    folded = jax.random.fold_in(key, 303)
    key_one, key_two = jax.random.split(folded, 2)
    query_block = jnp.arange(NQB, dtype=jnp.int32)
    upper_bound = jnp.minimum(query_block + 1, MAXB)
    counts = jax.random.randint(key_one, (SEQS, NQB), 1, upper_bound[None, :] + 1)
    counts = jnp.where(query_block[None, :] == NQB - 1, MAXB, counts).astype(jnp.int32)
    random_ints = jax.random.randint(key_two, (SEQS, NQB, NQB), 0, 1 << 20)
    column = jnp.arange(NQB, dtype=jnp.int32)
    sort_keys = random_ints * NQB + column[None, None, :]
    sort_keys = jnp.where(column[None, None, :] < query_block[None, :, None], sort_keys, (1 << 30) + column[None, None, :])
    picked = jnp.argsort(sort_keys, axis=2)[:, :, :MAXB - 1].astype(jnp.int32)
    own_block = jnp.broadcast_to(query_block[None, :, None], (SEQS, NQB, 1))
    slot_list = jnp.concatenate([own_block, picked], axis=2)
    slot_index = jnp.arange(MAXB, dtype=jnp.int32)
    slot_list = jnp.where(slot_index[None, None, :] < counts[:, :, None], slot_list, query_block[None, :, None])
    return (slot_list.astype(jnp.int32), counts)


def draw_key_blocks(key, part):
    return block_lists(key)[0]


def draw_block_counts(key, part):
    return block_lists(key)[1]


def shard_levels(key, dims, cuts, least, high):
    level, own = 1.0, jax.random.fold_in(key, 6)
    for dim, parts in cuts:
        steps = jnp.exp(jax.random.uniform(jax.random.fold_in(own, dim), (parts,), jnp.float32, least / len(cuts), high / len(cuts)))
        level = level * jnp.repeat(steps, dims[dim] // parts).reshape([-1 if axis == dim else 1 for axis in range(len(dims))])
    return level


def scatter_about(stream_key, dims, spread, limit, shards=(), kind=jnp.bfloat16):
    drawn = spread * jax.random.normal(stream_key, dims, jnp.float32)
    if shards:
        drawn = drawn * shard_levels(stream_key, dims, shards, -0.22, 0.18)
    return jnp.clip(drawn, -limit, limit).astype(kind)


def setup_inputs(seed: int = 0, part: int = 0) -> dict:
    arg_keys = jax.random.split(jax.random.key(seed), 8)
    own_keys = jax.random.split(jax.random.fold_in(arg_keys[7], part), 8)
    return {
        "queries": draw_queries(jax.random.fold_in(jax.random.fold_in(arg_keys[7], part), 71), part),
        "grad_out": scatter_about(own_keys[1], (SEQS, L, HP, 2 * VD), 1.0, 6.0, ((0, 2), (1, 4), (3, 2))),
        "latent_kv": draw_latent_kv(jax.random.fold_in(jax.random.fold_in(arg_keys[7], part), 71), part),
        "key_up": scatter_about(arg_keys[3], (HP, 2, NOPE, LAT), LAT ** -0.5, 0.25, ((0, 4), (1, 2))),
        "value_up": scatter_about(arg_keys[4], (HP, 2, LAT, VD), LAT ** -0.5, 0.25, ((0, 4), (1, 2))),
        "key_blocks": draw_key_blocks(jax.random.fold_in(jax.random.fold_in(arg_keys[7], part), 71), part),
        "block_counts": draw_block_counts(jax.random.fold_in(jax.random.fold_in(arg_keys[7], part), 71), part),
    }


def head_backward(head_queries, head_grads, latent, key_weight, value_weight, slot_list, count_list, block_rows):
    length = head_queries.shape[0]
    latent_width = key_weight.shape[1]
    nope_width = key_weight.shape[0]
    query_width = head_queries.shape[1]
    value_width = head_grads.shape[1]
    block_count = length // block_rows
    slot_count = slot_list.shape[1]
    factor = 1.0 / math.sqrt(query_width)
    compressed = latent[:, :latent_width]
    key_nope = jnp.dot(compressed, key_weight.T, preferred_element_type=jnp.float32).astype(jnp.bfloat16)
    values = jnp.dot(compressed, value_weight, preferred_element_type=jnp.float32).astype(jnp.bfloat16)
    keys_all = jnp.concatenate([key_nope, latent[:, latent_width:]], axis=1)
    key_tiles = keys_all.reshape(block_count, block_rows, query_width)
    value_tiles = values.reshape(block_count, block_rows, value_width)
    causal = lax.broadcasted_iota(jnp.int32, (block_rows, block_rows), 0) >= lax.broadcasted_iota(jnp.int32, (block_rows, block_rows), 1)
    slot_range = jnp.arange(slot_count, dtype=jnp.int32)

    def one_block(carry, inputs):
        key_total, value_total = carry
        query_tile, grad_tile, block_slots, block_live, block_index = inputs
        keys_here = key_tiles[block_slots].reshape(slot_count * block_rows, query_width).astype(jnp.float32)
        values_here = value_tiles[block_slots].reshape(slot_count * block_rows, value_width).astype(jnp.float32)
        live = slot_range < block_live
        diagonal = block_slots == block_index
        allowed = live[None, :, None] & (jnp.logical_not(diagonal)[None, :, None] | causal[:, None, :])
        allowed = allowed.reshape(block_rows, slot_count * block_rows)
        query_wide = query_tile.astype(jnp.float32)
        grad_wide = grad_tile.astype(jnp.float32)
        scores = jnp.einsum('qd,kd->qk', query_wide, keys_here) * factor
        scores = jnp.where(allowed, scores, -1e+30)
        top_score = lax.optimization_barrier(jnp.max(scores, axis=1, keepdims=True))
        expo = jnp.where(allowed, jnp.exp(scores - top_score), 0.0)
        probs = expo / lax.optimization_barrier(jnp.sum(expo, axis=1, keepdims=True))
        probs_b = probs.astype(jnp.bfloat16)
        probs_wide = probs_b.astype(jnp.float32)
        attended = jnp.einsum('qk,kd->qd', probs_wide, values_here)
        delta = lax.optimization_barrier(jnp.sum(grad_wide * attended, axis=1, keepdims=True))
        grad_probs = jnp.einsum('qd,kd->qk', grad_wide, values_here)
        grad_scores = (probs * (grad_probs - delta)).astype(jnp.bfloat16).astype(jnp.float32)
        grad_query = (jnp.einsum('qk,kd->qd', grad_scores, keys_here) * factor).astype(jnp.bfloat16)
        grad_key = jnp.einsum('qk,qd->kd', grad_scores, query_wide) * factor
        grad_value = jnp.einsum('qk,qd->kd', probs_wide, grad_wide)
        key_total = key_total.at[block_slots].add(grad_key.reshape(slot_count, block_rows, query_width))
        value_total = value_total.at[block_slots].add(grad_value.reshape(slot_count, block_rows, value_width))
        return ((key_total, value_total), grad_query)
    start = (jnp.zeros((block_count, block_rows, query_width), jnp.float32), jnp.zeros((block_count, block_rows, value_width), jnp.float32))
    inputs = (head_queries.reshape(block_count, block_rows, query_width), head_grads.reshape(block_count, block_rows, value_width), slot_list, count_list, jnp.arange(block_count, dtype=jnp.int32))
    (key_total, value_total), grad_tiles = lax.scan(one_block, start, inputs)
    grad_query = grad_tiles.reshape(length, query_width)
    key_grads = key_total.reshape(length, query_width)
    nope_grads = key_grads[:, :nope_width].astype(jnp.bfloat16)
    value_grads = value_total.reshape(length, value_width).astype(jnp.bfloat16)
    latent_grad = jnp.dot(nope_grads, key_weight, preferred_element_type=jnp.float32) + jnp.dot(value_grads, value_weight.T, preferred_element_type=jnp.float32)
    head_part = jnp.concatenate([latent_grad, key_grads[:, nope_width:]], axis=1).astype(jnp.bfloat16)
    key_weight_grad = jnp.dot(nope_grads.T, compressed, preferred_element_type=jnp.float32)
    value_weight_grad = jnp.dot(compressed.T, value_grads, preferred_element_type=jnp.float32)
    return (grad_query, head_part, key_weight_grad, value_weight_grad)

def reference(queries, grad_out, latent_kv, key_up, value_up, key_blocks, block_counts):
    head_total = 2 * HP
    key_flat = key_up.reshape(head_total, NOPE, LAT)
    value_flat = value_up.reshape(head_total, LAT, VD)
    query_list = []
    latent_list = []
    key_sum = jnp.zeros((head_total, NOPE, LAT), jnp.float32)
    value_sum = jnp.zeros((head_total, LAT, VD), jnp.float32)
    for sequence in range(queries.shape[0]):
        query_heads = jnp.transpose(queries[sequence].reshape(L, head_total, QD), (1, 0, 2))
        grad_heads = jnp.transpose(grad_out[sequence].reshape(L, head_total, VD), (1, 0, 2))
        latent = latent_kv[sequence]
        slot_list = key_blocks[sequence]
        count_list = block_counts[sequence]

        def one_head(total, inputs):
            head_q, head_g, key_weight, value_weight = inputs
            grad_query, head_part, key_weight_grad, value_weight_grad = head_backward(head_q, head_g, latent, key_weight, value_weight, slot_list, count_list, BLK)
            return (total + head_part.astype(jnp.float32), (grad_query, key_weight_grad, value_weight_grad))
        latent_total, (query_grads, key_grads, value_grads) = lax.scan(one_head, jnp.zeros((L, KVW), jnp.float32), (query_heads, grad_heads, key_flat, value_flat))
        query_list.append(jnp.transpose(query_grads, (1, 0, 2)).reshape(L, HP, 2 * QD))
        latent_list.append(latent_total)
        key_sum = key_sum + key_grads
        value_sum = value_sum + value_grads
    return (jnp.stack(query_list), jnp.stack(latent_list), key_sum.reshape(HP, 2, NOPE, LAT), value_sum.reshape(HP, 2, LAT, VD))
```

```python
import functools
import math

import jax
import jax.numpy as jnp
from jax import lax
from jax.experimental import pallas as pl
from jax.experimental.pallas import tpu as pltpu
from jax.sharding import PartitionSpec as P

BLK = 128
NN = (((1,), (0,)), ((), ()))
NT = (((1,), (1,)), ((), ()))


def mm(a, b, dims=NN):
    return lax.dot_general(a, b, dims, preferred_element_type=jnp.float32)


def head_math(q2, g2, k_w, v_w, lat_t, lat, bias, keys, keys_t):
    nope, width = k_w.shape
    query_width = keys_t.shape[0]
    factor = 1.0 / math.sqrt(query_width)
    keys[:, :nope] = mm(lat[...], k_w, NT).astype(jnp.bfloat16)
    keys_t[:nope, :] = mm(k_w, lat_t[:width, :]).astype(jnp.bfloat16)
    values = mm(lat[...], v_w).astype(jnp.bfloat16)
    scores = mm(keys[:, :query_width], q2) * factor + bias[...]
    expo = jnp.exp(scores - jnp.max(scores, axis=0, keepdims=True))
    probs = expo * (1.0 / jnp.sum(expo, axis=0, keepdims=True))
    probs_b = probs.astype(jnp.bfloat16)
    grad_probs = mm(values, g2, NT)
    delta = jnp.sum(probs_b.astype(jnp.float32) * grad_probs, axis=0, keepdims=True)
    grad_scores = (probs * (grad_probs - delta)).astype(jnp.bfloat16)
    dq = (mm(keys_t[...], grad_scores) * factor).astype(jnp.bfloat16)
    dk = mm(q2, grad_scores, NT) * factor
    value_b = mm(probs_b, g2).astype(jnp.bfloat16)
    nope_b = dk[:nope].astype(jnp.bfloat16)
    latent_part = mm(k_w.T, nope_b) + mm(v_w, value_b, NT)
    k_grad = mm(nope_b, lat_t[:width, :], NT)
    v_grad = mm(lat_t[:width, :], value_b)
    return dq, latent_part, dk[nope:], k_grad, v_grad


ORDER = ((0, 0), (0, 1), (1, 0), (0, 2), (1, 1), (0, 3), (1, 2), (1, 3))
FROM_FAR = {0: (0,), 2: (1,), 3: (2,), 5: (3,)}
FROM_SIDE = {1: (0,), 3: (1,), 5: (2,), 6: (3,)}
SUMMED = {3: (0,), 5: (1,), 7: (2,)}
ROUTES = 4


def attention_kernel(
    heads,
    slots, counts, q_in, g_in, lat_in, k_in, v_in,
    dq_out, lat_out, dk_out, dv_out,
    q_buf, g_buf, lat_buf, wk, wv, dq_buf, lat_t, lat, bias, keys, keys_t, dlat,
    k_half, v_half, k_keep, v_keep, kx_out, kx_in, vx_out, vx_in, kz_out, kz_in, vz_out, vz_in,
    half_in, piece_out, piece_in, cross_out, cross_in,
    q_send, q_recv, g_send, g_recv, lat_send, lat_recv, share_send, share_recv, w_send, w_recv,
    dq_send, dq_recv, kx_sem, vx_sem, kz_sem, vz_sem, half_sem, piece_send, piece_recv, own_sem,
):
    me = lax.axis_index("seq")
    rep = lax.axis_index("rep")
    sub = lax.axis_index("sub")
    group = lax.axis_index("groups")
    kv_width, total = lat_t.shape
    width = lat.shape[1]
    nope = wk.shape[2]
    query_width = keys_t.shape[0]
    k_rows = nope // 2
    v_rows = width // 2
    half_rows = kv_width // 2
    pairs = heads // 2
    side = me // 2
    place = lax.rem(me, 2)
    near = me + 1 - 2 * place
    cross = lax.rem(me + 2, 4)
    diagonal = 3 - me
    lat_rows = pl.ds(pl.multiple_of(sub * half_rows, 16), half_rows)

    def remote(src, dst, send, recv, **where):
        return pltpu.make_async_remote_copy(
            src_ref=src, dst_ref=dst, send_sem=send, recv_sem=recv,
            device_id=where, device_id_type=pl.DeviceIdType.MESH,
        )

    def q_copy(kind, i):
        owner = jnp.where(kind == 0, near, diagonal)
        return remote(q_in.at[pl.ds(owner * heads + 2 * i, 2)], q_buf.at[kind, place, pl.ds(2 * i, 2)],
                      q_send.at[kind, i], q_recv.at[kind, i], seq=near)

    def g_copy(kind, i):
        owner = jnp.where(kind == 0, near, diagonal)
        return remote(g_in.at[pl.ds(owner * heads + 2 * i, 2)], g_buf.at[kind, place, pl.ds(2 * i, 2)],
                      g_send.at[kind, i], g_recv.at[kind, i], seq=near)

    def lat_copy(slot, src, source, target):
        return remote(src, lat_buf.at[source, lat_rows],
                      lat_send.at[slot], lat_recv.at[slot], seq=target)

    lat_near = lat_copy(0, lat_in.at[lat_rows], me, near)
    lat_cross = lat_copy(1, lat_in.at[lat_rows], me, cross)
    lat_relay = lat_copy(2, lat_buf.at[cross, lat_rows], cross, near)

    def share_copy(slot, source):
        return remote(lat_buf.at[source, lat_rows], lat_buf.at[source, lat_rows],
                      share_send.at[slot], share_recv.at[slot], sub=1 - sub)

    def w_copies(route, i):
        piece = 2 * rep + group
        if route == 3:
            piece = 2 * (1 - rep) + group
        where = ({"seq": cross}, {"rep": 1 - rep}, {"groups": 1 - group}, {"groups": 1 - group})[route]
        both = pl.ds(2 * i, 2)
        k_part = pl.ds(pl.multiple_of(piece * (nope // ROUTES), 16), nope // ROUTES)
        v_part = pl.ds(pl.multiple_of(piece * (width // ROUTES), 16), width // ROUTES)
        k_to, v_to = wk.at[1, both, k_part], wv.at[1, both, v_part]
        k_from, v_from = (k_in.at[both, k_part], v_in.at[both, v_part]) if route == 0 else (k_to, v_to)
        return [
            remote(k_from, k_to, w_send.at[route, 0, i], w_recv.at[route, 0, i], **where),
            remote(v_from, v_to, w_send.at[route, 1, i], w_recv.at[route, 1, i], **where),
        ]

    def dq_copy(kind, i):
        owner = jnp.where(kind == 0, me, cross)
        return remote(dq_buf.at[kind, pl.ds(2 * i, 2)], dq_out.at[pl.ds(owner * heads + 2 * i, 2)],
                      dq_send.at[kind, i], dq_recv.at[kind, i], seq=near)

    def x_copies(kind, h):
        return [
            remote(kx_out.at[kind, h], kx_in.at[kind, h], kx_sem.at[0, kind, h], kx_sem.at[1, kind, h],
                   rep=1 - rep),
            remote(vx_out.at[kind, h], vx_in.at[kind, h], vx_sem.at[0, kind, h], vx_sem.at[1, kind, h],
                   rep=1 - rep),
        ]

    def z_copies(h):
        return [
            remote(kz_out.at[h], kz_in.at[h], kz_sem.at[0, h], kz_sem.at[1, h], seq=cross),
            remote(vz_out.at[h], vz_in.at[h], vz_sem.at[0, h], vz_sem.at[1, h], seq=cross),
        ]

    barrier = pltpu.get_barrier_semaphore()
    others = ({"seq": near}, {"seq": cross}, {"rep": 1 - rep}, {"groups": 1 - group}, {"sub": 1 - sub})
    for where in others:
        pl.semaphore_signal(barrier, inc=1, device_id=where, device_id_type=pl.DeviceIdType.MESH)
    pl.semaphore_wait(barrier, len(others))

    @pl.when(side == 0)
    def _():
        lat_cross.start()

    lat_near.start()
    for i in range(pairs):
        for copy in w_copies(0, i):
            copy.start()
        for kind in range(2):
            q_copy(kind, i).start()
            g_copy(kind, i).start()

    own = pl.ds(me * heads, heads)
    over = pl.ds(cross * heads, heads)
    locals_ = [
        pltpu.make_async_copy(lat_in, lat_buf.at[me], own_sem.at[0]),
        pltpu.make_async_copy(q_in.at[own], q_buf.at[0, place], own_sem.at[1]),
        pltpu.make_async_copy(g_in.at[own], g_buf.at[0, place], own_sem.at[2]),
        pltpu.make_async_copy(k_in, wk.at[0], own_sem.at[3]),
        pltpu.make_async_copy(v_in, wv.at[0], own_sem.at[4]),
        pltpu.make_async_copy(q_in.at[over], q_buf.at[1, place], own_sem.at[5]),
        pltpu.make_async_copy(g_in.at[over], g_buf.at[1, place], own_sem.at[6]),
    ]
    for copy in locals_:
        copy.start()

    key_at = lax.broadcasted_iota(jnp.int32, (BLK, BLK), 0)
    query_at = lax.broadcasted_iota(jnp.int32, (BLK, BLK), 1)
    for key_block in range(total // BLK):
        for t in range(2):
            query_block = 2 * side + t
            hit = jnp.int32(0)
            for m in range(slots.shape[0]):
                same = (slots[m, query_block] == key_block) & (m < counts[query_block])
                hit = hit | same.astype(jnp.int32)
            wide = jnp.full((BLK, BLK), hit, jnp.int32) > 0
            wide = wide & (key_at + key_block * BLK <= query_at + query_block * BLK)
            bias[key_block * BLK : (key_block + 1) * BLK, t * BLK : (t + 1) * BLK] = jnp.where(
                wide, 0.0, -1e30).astype(jnp.float32)
    dlat[...] = jnp.zeros_like(dlat)
    for copy in locals_:
        copy.wait()

    def fill(b):
        columns = slice(b * BLK, (b + 1) * BLK)
        lat_t[:, columns] = lat_buf[b]
        lat[columns, :] = lat_buf[b, :width, :].T
        keys[columns, nope:query_width] = lat_buf[b, width:, :].T
        keys_t[nope:, columns] = lat_buf[b, width:, :]

    share_near, share_cross, share_diagonal = share_copy(0, near), share_copy(1, cross), share_copy(2, diagonal)

    @pl.when(side == 1)
    def _():
        lat_cross.wait_recv()
        lat_relay.start()
        share_cross.start()

    lat_near.wait()
    share_near.start()

    @pl.when(side == 0)
    def _():
        lat_cross.wait_send()
        share_near.wait()
        for b in range(2):
            fill(b)
        lat_t[:, 2 * BLK:] = jnp.zeros((kv_width, total - 2 * BLK), jnp.bfloat16)
        lat[2 * BLK:, :] = jnp.zeros((total - 2 * BLK, width), jnp.bfloat16)
        keys[2 * BLK:, nope:query_width] = jnp.zeros((total - 2 * BLK, query_width - nope), jnp.bfloat16)
        keys_t[nope:, 2 * BLK:] = jnp.zeros((query_width - nope, total - 2 * BLK), jnp.bfloat16)

    @pl.when(side == 1)
    def _():
        lat_relay.wait()
        share_diagonal.start()
        share_near.wait()
        share_cross.wait()
        share_diagonal.wait()
        for b in range(4):
            fill(b)

    def from_far(i):
        for copy in w_copies(0, i):
            copy.wait()
        for copy in w_copies(1, i) + w_copies(2, i):
            copy.start()

    def from_side(i):
        for copy in w_copies(1, i):
            copy.wait()
        for copy in w_copies(3, i):
            copy.start()

    def sum_pair(i):
        for h in (2 * i, 2 * i + 1):
            for copy in x_copies(1, h):
                copy.wait()
            kz_out[h] = (k_keep[1, h] + kx_in[1, h].astype(jnp.float32)).astype(jnp.bfloat16)
            vz_out[h] = (v_keep[1, h] + vx_in[1, h].astype(jnp.float32)).astype(jnp.bfloat16)
            for copy in z_copies(h):
                copy.start()

    def one_step(n, unused):
        kind = jnp.int32(0)
        i = jnp.int32(0)
        for at, (its_kind, its_pair) in enumerate(ORDER):
            kind = jnp.where(n == at, its_kind, kind)
            i = jnp.where(n == at, its_pair, i)

        for at in range(len(ORDER)):
            if at in FROM_FAR or at in FROM_SIDE:
                @pl.when(n == at)
                def _():
                    for pair in FROM_SIDE.get(at, ()):
                        from_side(pair)
                    for pair in FROM_FAR.get(at, ()):
                        from_far(pair)

        @pl.when(kind == 1)
        def _():
            for copy in w_copies(2, i) + w_copies(3, i):
                copy.wait()

        q_copy(kind, i).wait()
        g_copy(kind, i).wait()
        owner = jnp.where(kind == 0, me, cross)

        def one_head(c, unused):
            h = 2 * i + c
            q2 = jnp.concatenate([q_buf[kind, 0, h], q_buf[kind, 1, h]], axis=1)
            g2 = jnp.concatenate([g_buf[kind, 0, h], g_buf[kind, 1, h]], axis=0)
            dq, latent_part, rope, k_grad, v_grad = head_math(
                q2, g2, wk[kind, h], wv[kind, h], lat_t, lat, bias, keys, keys_t
            )
            dq_out[owner * heads + h] = jnp.where(place == 0, dq[:, :BLK], dq[:, BLK:])
            dq_buf[kind, h] = jnp.where(place == 0, dq[:, BLK:], dq[:, :BLK])
            dlat[:width, :] += latent_part
            dlat[width:, :] += rope
            k_half[...] = k_grad
            v_half[...] = v_grad
            kx_out[kind, h] = k_half[pl.ds((1 - rep) * k_rows, k_rows), :].astype(jnp.bfloat16)
            vx_out[kind, h] = v_half[pl.ds((1 - rep) * v_rows, v_rows), :].astype(jnp.bfloat16)
            for copy in x_copies(kind, h):
                copy.start()
            k_keep[kind, h] = k_half[pl.ds(rep * k_rows, k_rows), :]
            v_keep[kind, h] = v_half[pl.ds(rep * v_rows, v_rows), :]
            return unused

        lax.fori_loop(0, 2, one_head, 0)
        dq_copy(kind, i).start()

        for at, which in SUMMED.items():
            @pl.when(n == at)
            def _():
                for pair in which:
                    sum_pair(pair)

        return unused

    lax.fori_loop(0, len(ORDER), one_step, 0)

    exchange = remote(dlat.at[pl.ds((1 - sub) * half_rows, half_rows), :], half_in,
                      half_sem.at[0], half_sem.at[1], sub=1 - sub)
    exchange.start()
    sum_pair(pairs - 1)
    exchange.wait()
    half_in[...] += dlat[pl.ds(sub * half_rows, half_rows), :]

    def columns_of(block):
        return half_in[:, pl.ds(pl.multiple_of(block * BLK, BLK), BLK)]

    def piece(slot):
        return remote(piece_out.at[slot], piece_in.at[slot], piece_send.at[slot], piece_recv.at[slot], seq=near)

    across = remote(cross_out, cross_in, piece_send.at[2], piece_recv.at[2], seq=cross)
    piece_out[0] = columns_of(near).astype(jnp.bfloat16)
    piece(0).start()

    @pl.when(side == 1)
    def _():
        piece_out[1] = columns_of(diagonal).astype(jnp.bfloat16)
        piece(1).start()
        piece(1).wait()
        cross_out[...] = (columns_of(cross) + piece_in[1].astype(jnp.float32)).astype(jnp.bfloat16)
        across.start()

    piece(0).wait()
    lat_out[...] = columns_of(me) + piece_in[0].astype(jnp.float32)

    def finish(h, unused):
        for copy in x_copies(0, h) + z_copies(h):
            copy.wait()
        dk_out[h] = k_keep[0, h] + kx_in[0, h].astype(jnp.float32) + kz_in[h].astype(jnp.float32)
        dv_out[h] = v_keep[0, h] + vx_in[0, h].astype(jnp.float32) + vz_in[h].astype(jnp.float32)
        return unused

    lax.fori_loop(0, heads, finish, 0)

    @pl.when(side == 0)
    def _():
        across.wait_recv()
        lat_out[...] += cross_in[...].astype(jnp.float32)

    @pl.when(side == 1)
    def _():
        across.wait_send()

    for i in range(pairs):
        for kind in range(2):
            dq_copy(kind, i).wait()


def local_small(queries, grad_out, latent_kv, key_up, value_up, key_blocks, block_counts):
    shards = lax.axis_size("seq")
    heads, _, nope, width = key_up.shape
    value_width = value_up.shape[3]
    q_t = jnp.transpose(queries[0], (1, 2, 0))
    g_t = jnp.transpose(grad_out[0], (1, 0, 2))
    lat_local = latent_kv[0].T
    kv_width, tokens = lat_local.shape
    total = shards * tokens
    query_width = q_t.shape[1]
    half = kv_width // 2
    pairs = heads // 2
    bf16, f32 = jnp.bfloat16, jnp.float32
    hbm = pl.BlockSpec(memory_space=pl.ANY)
    vmem = pl.BlockSpec(memory_space=pltpu.VMEM)
    smem = pl.BlockSpec(memory_space=pltpu.SMEM)
    sems = lambda *shape: pltpu.SemaphoreType.DMA(shape)
    k_part, v_part = (nope // 2, width), (width // 2, value_width)
    dq, dlat, dk, dv = pl.pallas_call(
        functools.partial(attention_kernel, heads),
        in_specs=[smem, smem, hbm, hbm, hbm, hbm, hbm],
        out_specs=[vmem, vmem, vmem, vmem],
        out_shape=[
            jax.ShapeDtypeStruct(q_t.shape, bf16),
            jax.ShapeDtypeStruct((half, tokens), f32),
            jax.ShapeDtypeStruct((heads, *k_part), f32),
            jax.ShapeDtypeStruct((heads, *v_part), f32),
        ],
        scratch_shapes=[
            pltpu.VMEM((2, 2, heads, query_width, tokens), bf16),
            pltpu.VMEM((2, 2, heads, tokens, value_width), bf16),
            pltpu.VMEM((shards, kv_width, tokens), bf16),
            pltpu.VMEM((2, heads, nope, width), bf16),
            pltpu.VMEM((2, heads, width, value_width), bf16),
            pltpu.VMEM((2, heads, query_width, tokens), bf16),
            pltpu.VMEM((kv_width, total), bf16),
            pltpu.VMEM((total, width), bf16),
            pltpu.VMEM((total, 2 * BLK), f32),
            pltpu.VMEM((total, 2 * BLK), bf16),
            pltpu.VMEM((query_width, total), bf16),
            pltpu.VMEM((kv_width, total), f32),
            pltpu.VMEM((nope, width), f32),
            pltpu.VMEM((width, value_width), f32),
            pltpu.VMEM((2, heads, *k_part), f32),
            pltpu.VMEM((2, heads, *v_part), f32),
            pltpu.VMEM((2, heads, *k_part), bf16),
            pltpu.VMEM((2, heads, *k_part), bf16),
            pltpu.VMEM((2, heads, *v_part), bf16),
            pltpu.VMEM((2, heads, *v_part), bf16),
            pltpu.VMEM((heads, *k_part), bf16),
            pltpu.VMEM((heads, *k_part), bf16),
            pltpu.VMEM((heads, *v_part), bf16),
            pltpu.VMEM((heads, *v_part), bf16),
            pltpu.VMEM((half, total), f32),
            pltpu.VMEM((2, half, tokens), bf16),
            pltpu.VMEM((2, half, tokens), bf16),
            pltpu.VMEM((half, tokens), bf16),
            pltpu.VMEM((half, tokens), bf16),
            sems(2, pairs), sems(2, pairs), sems(2, pairs), sems(2, pairs),
            sems(3), sems(3), sems(3), sems(3),
            sems(ROUTES, 2, pairs), sems(ROUTES, 2, pairs),
            sems(2, pairs), sems(2, pairs),
            sems(2, 2, heads), sems(2, 2, heads), sems(2, heads), sems(2, heads),
            sems(2), sems(3), sems(3), sems(7),
        ],
        compiler_params=pltpu.CompilerParams(
            collective_id=0, has_side_effects=True, vmem_limit_bytes=40 << 20
        ),
    )(key_blocks[0].T, block_counts[0], q_t, g_t, lat_local, key_up[:, 0], value_up[:, 0])
    return (
        jnp.transpose(dq, (2, 0, 1))[None],
        dlat.T[None],
        dk[:, None],
        dv[:, None],
    )


def head_backward(
    head_queries, head_grads, latent, key_weight, value_weight, slot_list, count_list, block_rows
):
    length = head_queries.shape[0]
    latent_width = key_weight.shape[1]
    nope_width = key_weight.shape[0]
    query_width = head_queries.shape[1]
    value_width = head_grads.shape[1]
    block_count = length // block_rows
    slot_count = slot_list.shape[1]
    factor = 1.0 / math.sqrt(query_width)
    compressed = latent[:, :latent_width]
    key_nope = jnp.einsum(
        "tl,dl->td", compressed, key_weight, preferred_element_type=jnp.float32
    ).astype(jnp.bfloat16)
    values = jnp.dot(compressed, value_weight, preferred_element_type=jnp.float32).astype(
        jnp.bfloat16
    )
    keys_all = jnp.concatenate([key_nope, latent[:, latent_width:]], axis=1)
    per_group = math.gcd(block_count, max(1, 512 // block_rows))
    group_count = block_count // per_group
    key_tiles = keys_all.reshape(block_count, block_rows, query_width)
    value_tiles = values.reshape(block_count, block_rows, value_width)
    causal = lax.broadcasted_iota(jnp.int32, (block_rows, block_rows), 0) >= lax.broadcasted_iota(
        jnp.int32, (block_rows, block_rows), 1
    )
    slot_range = jnp.arange(slot_count, dtype=jnp.int32)
    within = jnp.arange(per_group, dtype=jnp.int32)

    def tiles_at(tiles, group_slots):
        return jnp.stack([
            jnp.concatenate([
                lax.dynamic_index_in_dim(tiles, group_slots[b, m], 0, keepdims=False)
                for m in range(slot_count)
            ])
            for b in range(per_group)
        ])

    def one_group(carry, inputs):
        key_total, value_total = carry
        query_tile, grad_tile, group_slots, group_counts, group_index = inputs
        own_blocks = group_index * per_group + within
        keys_here = tiles_at(key_tiles, group_slots)
        values_here = tiles_at(value_tiles, group_slots)
        live = slot_range[None, :] < group_counts[:, None]
        diagonal = group_slots == own_blocks[:, None]
        allowed = live[:, None, :, None] & (
            jnp.logical_not(diagonal)[:, None, :, None] | causal[None, :, None, :]
        )
        allowed = allowed.reshape(per_group, block_rows, slot_count * block_rows)
        scores = (
            jnp.einsum("gqd,gkd->gqk", query_tile, keys_here, preferred_element_type=jnp.float32)
            * factor
        )
        scores = jnp.where(allowed, scores, -1e30)
        top_score = jnp.max(scores, axis=2, keepdims=True)
        expo = jnp.where(allowed, jnp.exp(scores - top_score), 0.0)
        probs = expo / jnp.sum(expo, axis=2, keepdims=True)
        probs_b = probs.astype(jnp.bfloat16)
        attended = jnp.einsum(
            "gqk,gkd->gqd", probs_b, values_here, preferred_element_type=jnp.float32
        )
        delta = jnp.sum(grad_tile.astype(jnp.float32) * attended, axis=2, keepdims=True)
        grad_probs = jnp.einsum(
            "gqd,gkd->gqk", grad_tile, values_here, preferred_element_type=jnp.float32
        )
        grad_scores = (probs * (grad_probs - delta)).astype(jnp.bfloat16)
        grad_query = (
            jnp.einsum("gqk,gkd->gqd", grad_scores, keys_here, preferred_element_type=jnp.float32)
            * factor
        ).astype(jnp.bfloat16)
        grad_key = (
            jnp.einsum("gqk,gqd->gkd", grad_scores, query_tile, preferred_element_type=jnp.float32)
            * factor
        )
        grad_value = jnp.einsum(
            "gqk,gqd->gkd", probs_b, grad_tile, preferred_element_type=jnp.float32
        )
        flat_slots = group_slots.reshape(per_group * slot_count)
        key_total = key_total.at[flat_slots].add(
            grad_key.reshape(per_group * slot_count, block_rows, query_width)
        )
        value_total = value_total.at[flat_slots].add(
            grad_value.reshape(per_group * slot_count, block_rows, value_width)
        )
        return ((key_total, value_total), grad_query)

    start = (
        jnp.zeros((block_count, block_rows, query_width), jnp.float32),
        jnp.zeros((block_count, block_rows, value_width), jnp.float32),
    )
    inputs = (
        head_queries.reshape(group_count, per_group, block_rows, query_width),
        head_grads.reshape(group_count, per_group, block_rows, value_width),
        slot_list.reshape(group_count, per_group, slot_count),
        count_list.reshape(group_count, per_group),
        jnp.arange(group_count, dtype=jnp.int32),
    )
    (key_total, value_total), grad_tiles = lax.scan(one_group, start, inputs)
    grad_query = grad_tiles.reshape(length, query_width)
    key_grads = key_total.reshape(length, query_width)
    nope_grads = key_grads[:, :nope_width].astype(jnp.bfloat16)
    value_grads = value_total.reshape(length, value_width).astype(jnp.bfloat16)
    latent_grad = jnp.dot(nope_grads, key_weight, preferred_element_type=jnp.float32) + jnp.einsum(
        "tv,lv->tl", value_grads, value_weight, preferred_element_type=jnp.float32
    )
    head_part = jnp.concatenate([latent_grad, key_grads[:, nope_width:]], axis=1).astype(
        jnp.bfloat16
    )
    key_weight_grad = jnp.einsum(
        "td,tl->dl", nope_grads, compressed, preferred_element_type=jnp.float32
    )
    value_weight_grad = jnp.einsum(
        "tl,tv->lv", compressed, value_grads, preferred_element_type=jnp.float32
    )
    return (grad_query, head_part, key_weight_grad, value_weight_grad)


def local_general(queries, grad_out, latent_kv, key_up, value_up, key_blocks, block_counts):
    head_queries, head_grads = (
        lax.all_to_all(queries, "seq", split_axis=2, concat_axis=1, tiled=True),
        lax.all_to_all(grad_out, "seq", split_axis=2, concat_axis=1, tiled=True),
    )
    latent = lax.all_gather(latent_kv, "seq", axis=1, tiled=True)[0]
    slot_list = key_blocks[0]
    count_list = block_counts[0]
    query_stack = jnp.moveaxis(head_queries[0], 1, 0)
    grad_stack = jnp.moveaxis(head_grads[0], 1, 0)

    def one_head(carry, inputs):
        head_q, head_g, key_weight, value_weight = inputs
        results = head_backward(
            head_q, head_g, latent, key_weight, value_weight, slot_list, count_list, BLK
        )
        return (carry, results)

    unused, (query_grads, head_parts, key_grads, value_grads) = lax.scan(
        one_head,
        jnp.zeros((), jnp.float32),
        (query_stack, grad_stack, key_up[:, 0], value_up[:, 0]),
    )
    returning = jnp.moveaxis(query_grads, 0, 1)[None]
    grad_queries = lax.all_to_all(returning, "seq", split_axis=1, concat_axis=2, tiled=True)
    heads_here, length, part_width = head_parts.shape
    seq_count = lax.axis_size("seq")
    tokens_here = length // seq_count
    pieces = head_parts.reshape(heads_here, seq_count, tokens_here, part_width)
    arrived = lax.all_to_all(pieces, "seq", split_axis=1, concat_axis=1, tiled=True)
    summed = jnp.sum(arrived.astype(jnp.float32), axis=(0, 1))
    grad_latent = lax.psum_scatter(summed, "sub", scatter_dimension=1, tiled=True)
    key_grads = key_grads[:, None]
    value_grads = value_grads[:, None]
    total_key, total_value = lax.psum((key_grads, value_grads), "rep")
    replica_count = lax.axis_size("rep")
    replica_index = lax.axis_index("rep")
    key_rows = total_key.shape[2] // replica_count
    value_rows = total_value.shape[2] // replica_count
    grad_key_up = lax.dynamic_slice_in_dim(total_key, replica_index * key_rows, key_rows, 2)
    grad_value_up = lax.dynamic_slice_in_dim(total_value, replica_index * value_rows, value_rows, 2)
    return (grad_queries, grad_latent[None], grad_key_up, grad_value_up)


def solution(mesh):
    placed = (
        P(("groups", "rep"), "seq", None, "sub"),
        P(("groups", "rep"), "seq", None, "sub"),
        P(("groups", "rep"), "seq", None),
        P("seq", "sub", None, None),
        P("seq", "sub", None, None),
        P(("groups", "rep"), None, None),
        P(("groups", "rep"), None),
    )

    def local(queries, grad_out, latent_kv, key_up, value_up, key_blocks, block_counts):
        args = (queries, grad_out, latent_kv, key_up, value_up, key_blocks, block_counts)
        shards = mesh.shape["seq"]
        small = (
            queries.shape[1] == BLK
            and shards == 4
            and mesh.shape["rep"] == 2
            and mesh.shape["sub"] == 2
            and mesh.shape["groups"] == 2
            and key_up.shape[0] == 8
            and latent_kv.shape[2] % 32 == 0
        )
        return local_small(*args) if small else local_general(*args)

    return jax.shard_map(
        local,
        mesh=mesh,
        in_specs=placed,
        out_specs=(
            P(("groups", "rep"), "seq", None, "sub"),
            P(("groups", "rep"), "seq", "sub"),
            P(("groups", "seq"), "sub", "rep", None),
            P(("groups", "seq"), "sub", "rep", None),
        ),
        check_vma=False,
    )
```

```python
import functools
import math

import jax
import jax.numpy as jnp
from jax import lax
from jax.experimental import pallas as pl
from jax.experimental.pallas import tpu as pltpu
from jax.sharding import PartitionSpec as P

BLK = 128
NN = (((1,), (0,)), ((), ()))
NT = (((1,), (1,)), ((), ()))


def mm(a, b, dims=NN):
    return lax.dot_general(a, b, dims, preferred_element_type=jnp.float32)


def head_math(q2, g2, k_w, v_w, lat_t, lat, bias, keys, keys_t):
    nope, width = k_w.shape
    query_width = keys_t.shape[0]
    factor = 1.0 / math.sqrt(query_width)
    keys[:, :nope] = mm(lat[...], k_w, NT).astype(jnp.bfloat16)
    keys_t[:nope, :] = mm(k_w, lat_t[:width, :]).astype(jnp.bfloat16)
    values = mm(lat[...], v_w).astype(jnp.bfloat16)
    scores = mm(keys[:, :query_width], q2) * factor + bias[...]
    expo = jnp.exp(scores - jnp.max(scores, axis=0, keepdims=True))
    probs = expo * (1.0 / jnp.sum(expo, axis=0, keepdims=True))
    probs_b = probs.astype(jnp.bfloat16)
    grad_probs = mm(values, g2, NT)
    delta = jnp.sum(probs_b.astype(jnp.float32) * grad_probs, axis=0, keepdims=True)
    grad_scores = (probs * (grad_probs - delta)).astype(jnp.bfloat16)
    dq = (mm(keys_t[...], grad_scores) * factor).astype(jnp.bfloat16)
    dk = mm(q2, grad_scores, NT) * factor
    value_b = mm(probs_b, g2).astype(jnp.bfloat16)
    nope_b = dk[:nope].astype(jnp.bfloat16)
    latent_part = mm(k_w.T, nope_b) + mm(v_w, value_b, NT)
    k_grad = mm(nope_b, lat_t[:width, :], NT)
    v_grad = mm(lat_t[:width, :], value_b)
    return dq, latent_part, dk[nope:], k_grad, v_grad


ORDER = ((0, 0), (1, 0), (1, 1), (1, 2), (1, 3), (0, 1), (0, 2), (0, 3))
FROM_FAR = {0: (0,), 1: (1,), 2: (2,), 3: (3,)}
SUMMED = {2: (0,), 3: (1,), 4: (2,), 5: (3,)}
ROUTES = 4
AHEAD = 5
OWN_FROM = 5


def attention_kernel(
    heads,
    slots, counts, q_in, g_in, lat_in, k_in, v_in,
    dq_out, lat_out, dk_out, dv_out,
    q_buf, g_buf, lat_buf, wk, wv, dq_buf, lat_t, lat, bias, keys, keys_t, dlat,
    k_half, v_half, k_keep, v_keep, kx_out, kx_in, vx_out, vx_in, kz_out, kz_in, vz_out, vz_in,
    half_in, piece_out, piece_in, cross_out, cross_in,
    q_send, q_recv, g_send, g_recv, lat_send, lat_recv, share_send, share_recv, w_send, w_recv,
    dq_send, dq_recv, kx_sem, vx_sem, kz_sem, vz_sem, half_sem, piece_send, piece_recv, own_sem,
):
    me = lax.axis_index("seq")
    rep = lax.axis_index("rep")
    sub = lax.axis_index("sub")
    group = lax.axis_index("groups")
    kv_width, total = lat_t.shape
    width = lat.shape[1]
    nope = wk.shape[2]
    query_width = keys_t.shape[0]
    k_rows = nope // 2
    v_rows = width // 2
    half_rows = kv_width // 2
    pairs = heads // 2
    side = me // 2
    place = lax.rem(me, 2)
    near = me + 1 - 2 * place
    cross = lax.rem(me + 2, 4)
    diagonal = 3 - me
    lat_rows = pl.ds(pl.multiple_of(sub * half_rows, 16), half_rows)

    def remote(src, dst, send, recv, **where):
        return pltpu.make_async_remote_copy(
            src_ref=src, dst_ref=dst, send_sem=send, recv_sem=recv,
            device_id=where, device_id_type=pl.DeviceIdType.MESH,
        )

    def q_copy(kind, i):
        owner = jnp.where(kind == 0, near, diagonal)
        return remote(q_in.at[pl.ds(owner * heads + 2 * i, 2)], q_buf.at[kind, place, pl.ds(2 * i, 2)],
                      q_send.at[kind, i], q_recv.at[kind, i], seq=near)

    def g_copy(kind, i):
        owner = jnp.where(kind == 0, near, diagonal)
        return remote(g_in.at[pl.ds(owner * heads + 2 * i, 2)], g_buf.at[kind, place, pl.ds(2 * i, 2)],
                      g_send.at[kind, i], g_recv.at[kind, i], seq=near)

    def lat_copy(slot, src, source, target):
        return remote(src, lat_buf.at[source, lat_rows],
                      lat_send.at[slot], lat_recv.at[slot], seq=target)

    lat_near = lat_copy(0, lat_in.at[lat_rows], me, near)
    lat_cross = lat_copy(1, lat_in.at[lat_rows], me, cross)
    lat_relay = lat_copy(2, lat_buf.at[cross, lat_rows], cross, near)

    def share_copy(slot, source):
        return remote(lat_buf.at[source, lat_rows], lat_buf.at[source, lat_rows],
                      share_send.at[slot], share_recv.at[slot], sub=1 - sub)

    share_near, share_cross, share_diagonal = share_copy(0, near), share_copy(1, cross), share_copy(2, diagonal)

    def w_copies(route, i):
        piece = 2 * rep + group
        where = ({"seq": cross}, {"rep": 1 - rep}, {"groups": 1 - group},
                 {"rep": 1 - rep, "groups": 1 - group})[route]
        both = pl.ds(2 * i, 2)
        k_part = pl.ds(pl.multiple_of(piece * (nope // ROUTES), 16), nope // ROUTES)
        v_part = pl.ds(pl.multiple_of(piece * (width // ROUTES), 16), width // ROUTES)
        k_to, v_to = wk.at[1, both, k_part], wv.at[1, both, v_part]
        k_from, v_from = (k_in.at[both, k_part], v_in.at[both, v_part]) if route == 0 else (k_to, v_to)
        return [
            remote(k_from, k_to, w_send.at[route, 0, i], w_recv.at[route, 0, i], **where),
            remote(v_from, v_to, w_send.at[route, 1, i], w_recv.at[route, 1, i], **where),
        ]

    def dq_copy(kind, i):
        owner = jnp.where(kind == 0, me, cross)
        return remote(dq_buf.at[kind, pl.ds(2 * i, 2)], dq_out.at[pl.ds(owner * heads + 2 * i, 2)],
                      dq_send.at[kind, i], dq_recv.at[kind, i], seq=near)

    def x_copies(kind, h):
        return [
            remote(kx_out.at[kind, h], kx_in.at[kind, h], kx_sem.at[0, kind, h], kx_sem.at[1, kind, h],
                   rep=1 - rep),
            remote(vx_out.at[kind, h], vx_in.at[kind, h], vx_sem.at[0, kind, h], vx_sem.at[1, kind, h],
                   rep=1 - rep),
        ]

    def z_copies(h):
        return [
            remote(kz_out.at[h], kz_in.at[h], kz_sem.at[0, h], kz_sem.at[1, h], seq=cross),
            remote(vz_out.at[h], vz_in.at[h], vz_sem.at[0, h], vz_sem.at[1, h], seq=cross),
        ]

    own = pl.ds(me * heads, heads)
    over = pl.ds(cross * heads, heads)
    locals_ = [
        pltpu.make_async_copy(lat_in, lat_buf.at[me], own_sem.at[0]),
        pltpu.make_async_copy(q_in.at[own], q_buf.at[0, place], own_sem.at[1]),
        pltpu.make_async_copy(g_in.at[own], g_buf.at[0, place], own_sem.at[2]),
        pltpu.make_async_copy(k_in, wk.at[0], own_sem.at[3]),
        pltpu.make_async_copy(v_in, wv.at[0], own_sem.at[4]),
        pltpu.make_async_copy(q_in.at[over], q_buf.at[1, place], own_sem.at[5]),
        pltpu.make_async_copy(g_in.at[over], g_buf.at[1, place], own_sem.at[6]),
    ]
    for copy in locals_:
        copy.start()

    barrier = pltpu.get_barrier_semaphore()
    others = ({"seq": near}, {"seq": cross}, {"rep": 1 - rep}, {"groups": 1 - group},
              {"rep": 1 - rep, "groups": 1 - group}, {"sub": 1 - sub})
    for where in others:
        pl.semaphore_signal(barrier, inc=1, device_id=where, device_id_type=pl.DeviceIdType.MESH)
    pl.semaphore_wait(barrier, len(others))

    @pl.when(side == 0)
    def _():
        lat_cross.start()

    lat_near.start()
    for copy in w_copies(0, 0):
        copy.start()

    @pl.when(side == 1)
    def _():
        lat_cross.wait_recv()
        lat_relay.start()
        share_cross.start()

    for at in range(AHEAD):
        q_copy(*ORDER[at]).start()
        g_copy(*ORDER[at]).start()
        if at + 1 < pairs:
            for copy in w_copies(0, at + 1):
                copy.start()

    key_at = lax.broadcasted_iota(jnp.int32, (BLK, BLK), 0)
    query_at = lax.broadcasted_iota(jnp.int32, (BLK, BLK), 1)
    for key_block in range(total // BLK):
        for t in range(2):
            query_block = 2 * side + t
            hit = jnp.int32(0)
            for m in range(slots.shape[0]):
                same = (slots[m, query_block] == key_block) & (m < counts[query_block])
                hit = hit | same.astype(jnp.int32)
            wide = jnp.full((BLK, BLK), hit, jnp.int32) > 0
            wide = wide & (key_at + key_block * BLK <= query_at + query_block * BLK)
            bias[key_block * BLK : (key_block + 1) * BLK, t * BLK : (t + 1) * BLK] = jnp.where(
                wide, 0.0, -1e30).astype(jnp.float32)
    dlat[...] = jnp.zeros_like(dlat)
    for copy in locals_:
        copy.wait()

    def fill(b):
        columns = slice(b * BLK, (b + 1) * BLK)
        lat_t[:, columns] = lat_buf[b]
        lat[columns, :] = lat_buf[b, :width, :].T
        keys[columns, nope:query_width] = lat_buf[b, width:, :].T
        keys_t[nope:, columns] = lat_buf[b, width:, :]

    lat_near.wait()
    share_near.start()

    @pl.when(side == 0)
    def _():
        lat_cross.wait_send()
        share_near.wait()
        for b in range(2):
            fill(b)
        lat_t[:, 2 * BLK:] = jnp.zeros((kv_width, total - 2 * BLK), jnp.bfloat16)
        lat[2 * BLK:, :] = jnp.zeros((total - 2 * BLK, width), jnp.bfloat16)
        keys[2 * BLK:, nope:query_width] = jnp.zeros((total - 2 * BLK, query_width - nope), jnp.bfloat16)
        keys_t[nope:, 2 * BLK:] = jnp.zeros((query_width - nope, total - 2 * BLK), jnp.bfloat16)

    @pl.when(side == 1)
    def _():
        lat_relay.wait()
        share_diagonal.start()
        share_near.wait()
        share_cross.wait()
        share_diagonal.wait()
        for b in range(4):
            fill(b)

    def from_far(i):
        for copy in w_copies(0, i):
            copy.wait()
        for route in range(1, ROUTES):
            for copy in w_copies(route, i):
                copy.start()

    def sum_pair(i):
        for h in (2 * i, 2 * i + 1):
            for copy in x_copies(1, h):
                copy.wait()
            kz_out[h] = (k_keep[1, h] + kx_in[1, h].astype(jnp.float32)).astype(jnp.bfloat16)
            vz_out[h] = (v_keep[1, h] + vx_in[1, h].astype(jnp.float32)).astype(jnp.bfloat16)
            for copy in z_copies(h):
                copy.start()

    def one_step(n, unused):
        kind = jnp.int32(0)
        i = jnp.int32(0)
        for at, (its_kind, its_pair) in enumerate(ORDER):
            kind = jnp.where(n == at, its_kind, kind)
            i = jnp.where(n == at, its_pair, i)

        for at in range(len(ORDER) - AHEAD):
            @pl.when(n == at)
            def _():
                q_copy(*ORDER[at + AHEAD]).start()
                g_copy(*ORDER[at + AHEAD]).start()

        for at in range(len(ORDER)):
            if at in FROM_FAR:
                @pl.when(n == at)
                def _():
                    for pair in FROM_FAR.get(at, ()):
                        from_far(pair)

        @pl.when(kind == 1)
        def _():
            for route in range(1, ROUTES):
                for copy in w_copies(route, i):
                    copy.wait()

        q_copy(kind, i).wait()
        g_copy(kind, i).wait()
        owner = jnp.where(kind == 0, me, cross)

        def one_head(c, unused):
            h = 2 * i + c
            q2 = jnp.concatenate([q_buf[kind, 0, h], q_buf[kind, 1, h]], axis=1)
            g2 = jnp.concatenate([g_buf[kind, 0, h], g_buf[kind, 1, h]], axis=0)
            dq, latent_part, rope, k_grad, v_grad = head_math(
                q2, g2, wk[kind, h], wv[kind, h], lat_t, lat, bias, keys, keys_t
            )
            dq_out[owner * heads + h] = jnp.where(place == 0, dq[:, :BLK], dq[:, BLK:])
            dq_buf[kind, h] = jnp.where(place == 0, dq[:, BLK:], dq[:, :BLK])
            dlat[:width, :] += latent_part
            dlat[width:, :] += rope
            k_half[...] = k_grad
            v_half[...] = v_grad
            kx_out[kind, h] = k_half[pl.ds((1 - rep) * k_rows, k_rows), :].astype(jnp.bfloat16)
            vx_out[kind, h] = v_half[pl.ds((1 - rep) * v_rows, v_rows), :].astype(jnp.bfloat16)
            @pl.when(n > 0)
            def _():
                for copy in x_copies(kind, h):
                    copy.start()

            k_keep[kind, h] = k_half[pl.ds(rep * k_rows, k_rows), :]
            v_keep[kind, h] = v_half[pl.ds(rep * v_rows, v_rows), :]
            return unused

        lax.fori_loop(0, 2, one_head, 0)
        dq_copy(kind, i).start()

        for at, which in SUMMED.items():
            @pl.when(n == at)
            def _():
                for pair in which:
                    sum_pair(pair)
                if at == OWN_FROM - 1:
                    for h in range(2):
                        for copy in x_copies(0, h):
                            copy.start()

        return unused

    lax.fori_loop(0, len(ORDER), one_step, 0)

    exchange = remote(dlat.at[pl.ds((1 - sub) * half_rows, half_rows), :], half_in,
                      half_sem.at[0], half_sem.at[1], sub=1 - sub)
    exchange.start()
    exchange.wait()
    half_in[...] += dlat[pl.ds(sub * half_rows, half_rows), :]

    def columns_of(block):
        return half_in[:, pl.ds(pl.multiple_of(block * BLK, BLK), BLK)]

    def piece(slot):
        return remote(piece_out.at[slot], piece_in.at[slot], piece_send.at[slot], piece_recv.at[slot], seq=near)

    across = remote(cross_out, cross_in, piece_send.at[2], piece_recv.at[2], seq=cross)
    piece_out[0] = columns_of(near).astype(jnp.bfloat16)
    piece(0).start()

    @pl.when(side == 1)
    def _():
        piece_out[1] = columns_of(diagonal).astype(jnp.bfloat16)
        piece(1).start()
        piece(1).wait()
        cross_out[...] = (columns_of(cross) + piece_in[1].astype(jnp.float32)).astype(jnp.bfloat16)
        across.start()

    piece(0).wait()
    lat_out[...] = columns_of(me) + piece_in[0].astype(jnp.float32)

    def finish(h, unused):
        for copy in x_copies(0, h) + z_copies(h):
            copy.wait()
        dk_out[h] = k_keep[0, h] + kx_in[0, h].astype(jnp.float32) + kz_in[h].astype(jnp.float32)
        dv_out[h] = v_keep[0, h] + vx_in[0, h].astype(jnp.float32) + vz_in[h].astype(jnp.float32)
        return unused

    lax.fori_loop(0, heads, finish, 0)

    @pl.when(side == 0)
    def _():
        across.wait_recv()
        lat_out[...] += cross_in[...].astype(jnp.float32)

    @pl.when(side == 1)
    def _():
        across.wait_send()

    for i in range(pairs):
        for kind in range(2):
            dq_copy(kind, i).wait()


def local_small(queries, grad_out, latent_kv, key_up, value_up, key_blocks, block_counts):
    shards = lax.axis_size("seq")
    heads, _, nope, width = key_up.shape
    value_width = value_up.shape[3]
    q_t = jnp.transpose(queries[0], (1, 2, 0))
    g_t = jnp.transpose(grad_out[0], (1, 0, 2))
    lat_local = latent_kv[0].T
    kv_width, tokens = lat_local.shape
    total = shards * tokens
    query_width = q_t.shape[1]
    half = kv_width // 2
    pairs = heads // 2
    bf16, f32 = jnp.bfloat16, jnp.float32
    hbm = pl.BlockSpec(memory_space=pl.ANY)
    vmem = pl.BlockSpec(memory_space=pltpu.VMEM)
    smem = pl.BlockSpec(memory_space=pltpu.SMEM)
    sems = lambda *shape: pltpu.SemaphoreType.DMA(shape)
    k_part, v_part = (nope // 2, width), (width // 2, value_width)
    dq, dlat, dk, dv = pl.pallas_call(
        functools.partial(attention_kernel, heads),
        in_specs=[smem, smem, hbm, hbm, hbm, hbm, hbm],
        out_specs=[vmem, vmem, vmem, vmem],
        out_shape=[
            jax.ShapeDtypeStruct(q_t.shape, bf16),
            jax.ShapeDtypeStruct((half, tokens), f32),
            jax.ShapeDtypeStruct((heads, *k_part), f32),
            jax.ShapeDtypeStruct((heads, *v_part), f32),
        ],
        scratch_shapes=[
            pltpu.VMEM((2, 2, heads, query_width, tokens), bf16),
            pltpu.VMEM((2, 2, heads, tokens, value_width), bf16),
            pltpu.VMEM((shards, kv_width, tokens), bf16),
            pltpu.VMEM((2, heads, nope, width), bf16),
            pltpu.VMEM((2, heads, width, value_width), bf16),
            pltpu.VMEM((2, heads, query_width, tokens), bf16),
            pltpu.VMEM((kv_width, total), bf16),
            pltpu.VMEM((total, width), bf16),
            pltpu.VMEM((total, 2 * BLK), f32),
            pltpu.VMEM((total, 2 * BLK), bf16),
            pltpu.VMEM((query_width, total), bf16),
            pltpu.VMEM((kv_width, total), f32),
            pltpu.VMEM((nope, width), f32),
            pltpu.VMEM((width, value_width), f32),
            pltpu.VMEM((2, heads, *k_part), f32),
            pltpu.VMEM((2, heads, *v_part), f32),
            pltpu.VMEM((2, heads, *k_part), bf16),
            pltpu.VMEM((2, heads, *k_part), bf16),
            pltpu.VMEM((2, heads, *v_part), bf16),
            pltpu.VMEM((2, heads, *v_part), bf16),
            pltpu.VMEM((heads, *k_part), bf16),
            pltpu.VMEM((heads, *k_part), bf16),
            pltpu.VMEM((heads, *v_part), bf16),
            pltpu.VMEM((heads, *v_part), bf16),
            pltpu.VMEM((half, total), f32),
            pltpu.VMEM((2, half, tokens), bf16),
            pltpu.VMEM((2, half, tokens), bf16),
            pltpu.VMEM((half, tokens), bf16),
            pltpu.VMEM((half, tokens), bf16),
            sems(2, pairs), sems(2, pairs), sems(2, pairs), sems(2, pairs),
            sems(3), sems(3), sems(3), sems(3),
            sems(ROUTES, 2, pairs), sems(ROUTES, 2, pairs),
            sems(2, pairs), sems(2, pairs),
            sems(2, 2, heads), sems(2, 2, heads), sems(2, heads), sems(2, heads),
            sems(2), sems(3), sems(3), sems(7),
        ],
        compiler_params=pltpu.CompilerParams(
            collective_id=0, has_side_effects=True, vmem_limit_bytes=40 << 20
        ),
    )(key_blocks[0].T, block_counts[0], q_t, g_t, lat_local, key_up[:, 0], value_up[:, 0])
    return (
        jnp.transpose(dq, (2, 0, 1))[None],
        dlat.T[None],
        dk[:, None],
        dv[:, None],
    )


def head_backward(
    head_queries, head_grads, latent, key_weight, value_weight, slot_list, count_list, block_rows
):
    length = head_queries.shape[0]
    latent_width = key_weight.shape[1]
    nope_width = key_weight.shape[0]
    query_width = head_queries.shape[1]
    value_width = head_grads.shape[1]
    block_count = length // block_rows
    slot_count = slot_list.shape[1]
    factor = 1.0 / math.sqrt(query_width)
    compressed = latent[:, :latent_width]
    key_nope = jnp.einsum(
        "tl,dl->td", compressed, key_weight, preferred_element_type=jnp.float32
    ).astype(jnp.bfloat16)
    values = jnp.dot(compressed, value_weight, preferred_element_type=jnp.float32).astype(
        jnp.bfloat16
    )
    keys_all = jnp.concatenate([key_nope, latent[:, latent_width:]], axis=1)
    per_group = math.gcd(block_count, max(1, 512 // block_rows))
    group_count = block_count // per_group
    key_tiles = keys_all.reshape(block_count, block_rows, query_width)
    value_tiles = values.reshape(block_count, block_rows, value_width)
    causal = lax.broadcasted_iota(jnp.int32, (block_rows, block_rows), 0) >= lax.broadcasted_iota(
        jnp.int32, (block_rows, block_rows), 1
    )
    slot_range = jnp.arange(slot_count, dtype=jnp.int32)
    within = jnp.arange(per_group, dtype=jnp.int32)

    def tiles_at(tiles, group_slots):
        return jnp.stack([
            jnp.concatenate([
                lax.dynamic_index_in_dim(tiles, group_slots[b, m], 0, keepdims=False)
                for m in range(slot_count)
            ])
            for b in range(per_group)
        ])

    def one_group(carry, inputs):
        key_total, value_total = carry
        query_tile, grad_tile, group_slots, group_counts, group_index = inputs
        own_blocks = group_index * per_group + within
        keys_here = tiles_at(key_tiles, group_slots)
        values_here = tiles_at(value_tiles, group_slots)
        live = slot_range[None, :] < group_counts[:, None]
        diagonal = group_slots == own_blocks[:, None]
        allowed = live[:, None, :, None] & (
            jnp.logical_not(diagonal)[:, None, :, None] | causal[None, :, None, :]
        )
        allowed = allowed.reshape(per_group, block_rows, slot_count * block_rows)
        scores = (
            jnp.einsum("gqd,gkd->gqk", query_tile, keys_here, preferred_element_type=jnp.float32)
            * factor
        )
        scores = jnp.where(allowed, scores, -1e30)
        top_score = jnp.max(scores, axis=2, keepdims=True)
        expo = jnp.where(allowed, jnp.exp(scores - top_score), 0.0)
        probs = expo / jnp.sum(expo, axis=2, keepdims=True)
        probs_b = probs.astype(jnp.bfloat16)
        attended = jnp.einsum(
            "gqk,gkd->gqd", probs_b, values_here, preferred_element_type=jnp.float32
        )
        delta = jnp.sum(grad_tile.astype(jnp.float32) * attended, axis=2, keepdims=True)
        grad_probs = jnp.einsum(
            "gqd,gkd->gqk", grad_tile, values_here, preferred_element_type=jnp.float32
        )
        grad_scores = (probs * (grad_probs - delta)).astype(jnp.bfloat16)
        grad_query = (
            jnp.einsum("gqk,gkd->gqd", grad_scores, keys_here, preferred_element_type=jnp.float32)
            * factor
        ).astype(jnp.bfloat16)
        grad_key = (
            jnp.einsum("gqk,gqd->gkd", grad_scores, query_tile, preferred_element_type=jnp.float32)
            * factor
        )
        grad_value = jnp.einsum(
            "gqk,gqd->gkd", probs_b, grad_tile, preferred_element_type=jnp.float32
        )
        flat_slots = group_slots.reshape(per_group * slot_count)
        key_total = key_total.at[flat_slots].add(
            grad_key.reshape(per_group * slot_count, block_rows, query_width)
        )
        value_total = value_total.at[flat_slots].add(
            grad_value.reshape(per_group * slot_count, block_rows, value_width)
        )
        return ((key_total, value_total), grad_query)

    start = (
        jnp.zeros((block_count, block_rows, query_width), jnp.float32),
        jnp.zeros((block_count, block_rows, value_width), jnp.float32),
    )
    inputs = (
        head_queries.reshape(group_count, per_group, block_rows, query_width),
        head_grads.reshape(group_count, per_group, block_rows, value_width),
        slot_list.reshape(group_count, per_group, slot_count),
        count_list.reshape(group_count, per_group),
        jnp.arange(group_count, dtype=jnp.int32),
    )
    (key_total, value_total), grad_tiles = lax.scan(one_group, start, inputs)
    grad_query = grad_tiles.reshape(length, query_width)
    key_grads = key_total.reshape(length, query_width)
    nope_grads = key_grads[:, :nope_width].astype(jnp.bfloat16)
    value_grads = value_total.reshape(length, value_width).astype(jnp.bfloat16)
    latent_grad = jnp.dot(nope_grads, key_weight, preferred_element_type=jnp.float32) + jnp.einsum(
        "tv,lv->tl", value_grads, value_weight, preferred_element_type=jnp.float32
    )
    head_part = jnp.concatenate([latent_grad, key_grads[:, nope_width:]], axis=1).astype(
        jnp.bfloat16
    )
    key_weight_grad = jnp.einsum(
        "td,tl->dl", nope_grads, compressed, preferred_element_type=jnp.float32
    )
    value_weight_grad = jnp.einsum(
        "tl,tv->lv", compressed, value_grads, preferred_element_type=jnp.float32
    )
    return (grad_query, head_part, key_weight_grad, value_weight_grad)


def local_general(queries, grad_out, latent_kv, key_up, value_up, key_blocks, block_counts):
    head_queries, head_grads = (
        lax.all_to_all(queries, "seq", split_axis=2, concat_axis=1, tiled=True),
        lax.all_to_all(grad_out, "seq", split_axis=2, concat_axis=1, tiled=True),
    )
    latent = lax.all_gather(latent_kv, "seq", axis=1, tiled=True)[0]
    slot_list = key_blocks[0]
    count_list = block_counts[0]
    query_stack = jnp.moveaxis(head_queries[0], 1, 0)
    grad_stack = jnp.moveaxis(head_grads[0], 1, 0)

    def one_head(carry, inputs):
        head_q, head_g, key_weight, value_weight = inputs
        results = head_backward(
            head_q, head_g, latent, key_weight, value_weight, slot_list, count_list, BLK
        )
        return (carry, results)

    unused, (query_grads, head_parts, key_grads, value_grads) = lax.scan(
        one_head,
        jnp.zeros((), jnp.float32),
        (query_stack, grad_stack, key_up[:, 0], value_up[:, 0]),
    )
    returning = jnp.moveaxis(query_grads, 0, 1)[None]
    grad_queries = lax.all_to_all(returning, "seq", split_axis=1, concat_axis=2, tiled=True)
    heads_here, length, part_width = head_parts.shape
    seq_count = lax.axis_size("seq")
    tokens_here = length // seq_count
    pieces = head_parts.reshape(heads_here, seq_count, tokens_here, part_width)
    arrived = lax.all_to_all(pieces, "seq", split_axis=1, concat_axis=1, tiled=True)
    summed = jnp.sum(arrived.astype(jnp.float32), axis=(0, 1))
    grad_latent = lax.psum_scatter(summed, "sub", scatter_dimension=1, tiled=True)
    key_grads = key_grads[:, None]
    value_grads = value_grads[:, None]
    total_key, total_value = lax.psum((key_grads, value_grads), "rep")
    replica_count = lax.axis_size("rep")
    replica_index = lax.axis_index("rep")
    key_rows = total_key.shape[2] // replica_count
    value_rows = total_value.shape[2] // replica_count
    grad_key_up = lax.dynamic_slice_in_dim(total_key, replica_index * key_rows, key_rows, 2)
    grad_value_up = lax.dynamic_slice_in_dim(total_value, replica_index * value_rows, value_rows, 2)
    return (grad_queries, grad_latent[None], grad_key_up, grad_value_up)


def solution(mesh):
    placed = (
        P(("groups", "rep"), "seq", None, "sub"),
        P(("groups", "rep"), "seq", None, "sub"),
        P(("groups", "rep"), "seq", None),
        P("seq", "sub", None, None),
        P("seq", "sub", None, None),
        P(("groups", "rep"), None, None),
        P(("groups", "rep"), None),
    )

    def local(queries, grad_out, latent_kv, key_up, value_up, key_blocks, block_counts):
        args = (queries, grad_out, latent_kv, key_up, value_up, key_blocks, block_counts)
        shards = mesh.shape["seq"]
        small = (
            queries.shape[1] == BLK
            and shards == 4
            and mesh.shape["rep"] == 2
            and mesh.shape["sub"] == 2
            and mesh.shape["groups"] == 2
            and key_up.shape[0] == 8
            and latent_kv.shape[2] % 32 == 0
        )
        return local_small(*args) if small else local_general(*args)

    return jax.shard_map(
        local,
        mesh=mesh,
        in_specs=placed,
        out_specs=(
            P(("groups", "rep"), "seq", None, "sub"),
            P(("groups", "rep"), "seq", "sub"),
            P(("groups", "seq"), "sub", "rep", None),
            P(("groups", "seq"), "sub", "rep", None),
        ),
        check_vma=False,
    )
```

```python
import functools
import math

import jax
import jax.numpy as jnp
from jax import lax
from jax.experimental import pallas as pl
from jax.experimental.pallas import tpu as pltpu
from jax.sharding import PartitionSpec as P

BLK = 128
NN = (((1,), (0,)), ((), ()))
NT = (((1,), (1,)), ((), ()))


def mm(a, b, dims=NN):
    return lax.dot_general(a, b, dims, preferred_element_type=jnp.float32)


def head_math(q2, g2, k_w, v_w, lat_t, lat, bias, keys, keys_t):
    nope, width = k_w.shape
    query_width = keys_t.shape[0]
    factor = 1.0 / math.sqrt(query_width)
    keys[:, :nope] = mm(lat[...], k_w, NT).astype(jnp.bfloat16)
    keys_t[:nope, :] = mm(k_w, lat_t[:width, :]).astype(jnp.bfloat16)
    values = mm(lat[...], v_w).astype(jnp.bfloat16)
    scores = mm(keys[:, :query_width], q2) * factor + bias[...]
    expo = jnp.exp(scores - jnp.max(scores, axis=0, keepdims=True))
    probs = expo * (1.0 / jnp.sum(expo, axis=0, keepdims=True))
    probs_b = probs.astype(jnp.bfloat16)
    grad_probs = mm(values, g2, NT)
    delta = jnp.sum(probs_b.astype(jnp.float32) * grad_probs, axis=0, keepdims=True)
    grad_scores = (probs * (grad_probs - delta)).astype(jnp.bfloat16)
    dq = (mm(keys_t[...], grad_scores) * factor).astype(jnp.bfloat16)
    dk = mm(q2, grad_scores, NT) * factor
    value_b = mm(probs_b, g2).astype(jnp.bfloat16)
    nope_b = dk[:nope].astype(jnp.bfloat16)
    latent_part = mm(k_w.T, nope_b) + mm(v_w, value_b, NT)
    k_grad = mm(nope_b, lat_t[:width, :], NT)
    v_grad = mm(lat_t[:width, :], value_b)
    return dq, latent_part, dk[nope:], k_grad, v_grad


PAIRS = 4
EXTRA = 1
KEPT = PAIRS - EXTRA
SLOTS = tuple((1, i) for i in range(PAIRS)) + tuple((2, i) for i in range(EXTRA))
TASKS = ((0, 0), (0, 1)) + SLOTS + ((0, 2), (0, 3))
LAST_SLOT = len(SLOTS) + 1
ROUTES = 4
AHEAD = 4


def inner_only(kind, i):
    return kind == 2 or (kind == 1 and i >= KEPT)


def attention_kernel(
    heads,
    slots, counts, q_in, g_in, lat_in, k_in, v_in,
    dq_out, lat_out, dk_out, dv_out,
    q_buf, g_buf, lat_buf, wk, wv, dq_buf, lat_t, lat, bias, keys, keys_t, dlat,
    k_half, v_half, k_keep, v_keep, kx_out, kx_in, vx_out, vx_in, kz_out, kz_in, vz_out, vz_in,
    half_in, piece_out, piece_in, cross_out, cross_in,
    q_send, q_recv, g_send, g_recv, lat_send, lat_recv, share_send, share_recv, w_send, w_recv,
    dq_send, dq_recv, kx_sem, vx_sem, kz_send, kz_recv, vz_send, vz_recv, half_sem, piece_send, piece_recv, own_sem,
):
    me = lax.axis_index("seq")
    rep = lax.axis_index("rep")
    sub = lax.axis_index("sub")
    group = lax.axis_index("groups")
    kv_width, total = lat_t.shape
    width = lat.shape[1]
    nope = wk.shape[2]
    query_width = keys_t.shape[0]
    k_rows = nope // 2
    v_rows = width // 2
    half_rows = kv_width // 2
    side = me // 2
    place = lax.rem(me, 2)
    near = me + 1 - 2 * place
    cross = lax.rem(me + 2, 4)
    diagonal = 3 - me
    inner = (me == 1) | (me == 2)
    outer = jnp.logical_not(inner)
    lat_rows = pl.ds(pl.multiple_of(sub * half_rows, 16), half_rows)

    def remote(src, dst, send, recv, **where):
        return pltpu.make_async_remote_copy(
            src_ref=src, dst_ref=dst, send_sem=send, recv_sem=recv,
            device_id=where, device_id_type=pl.DeviceIdType.MESH,
        )

    def first_head(kind, i):
        return jnp.where(kind == 2, 2 * (KEPT + i), 2 * i)

    def near_rows(kind, i):
        owner = jnp.where(kind == 0, near, jnp.where(kind == 1, diagonal, cross))
        return pl.ds(owner * heads + first_head(kind, i), 2)

    def q_copy(kind, i):
        return remote(q_in.at[near_rows(kind, i)], q_buf.at[kind, place, pl.ds(2 * i, 2)],
                      q_send.at[kind, i], q_recv.at[kind, i], seq=near)

    def g_copy(kind, i):
        return remote(g_in.at[near_rows(kind, i)], g_buf.at[kind, place, pl.ds(2 * i, 2)],
                      g_send.at[kind, i], g_recv.at[kind, i], seq=near)

    def on(condition, needed, act):
        if needed:
            pl.when(condition)(act)
        else:
            act()

    def send_task(kind, i):
        def act():
            q_copy(kind, i).start()
            g_copy(kind, i).start()
        on(outer, inner_only(kind, i), act)

    def lat_copy(slot, src, source, target):
        return remote(src, lat_buf.at[source, lat_rows],
                      lat_send.at[slot], lat_recv.at[slot], seq=target)

    lat_near = lat_copy(0, lat_in.at[lat_rows], me, near)
    lat_cross = lat_copy(1, lat_in.at[lat_rows], me, cross)
    lat_relay = lat_copy(2, lat_buf.at[cross, lat_rows], cross, near)

    def share_copy(slot, source):
        return remote(lat_buf.at[source, lat_rows], lat_buf.at[source, lat_rows],
                      share_send.at[slot], share_recv.at[slot], sub=1 - sub)

    share_near, share_cross, share_diagonal = share_copy(0, near), share_copy(1, cross), share_copy(2, diagonal)

    def w_copies(route, slot, kind, i, source, where):
        piece = 2 * rep + group
        k_part = pl.ds(pl.multiple_of(piece * (nope // ROUTES), 16), nope // ROUTES)
        v_part = pl.ds(pl.multiple_of(piece * (width // ROUTES), 16), width // ROUTES)
        k_to, v_to = wk.at[kind, pl.ds(2 * i, 2), k_part], wv.at[kind, pl.ds(2 * i, 2), v_part]
        if source is None:
            k_from, v_from = k_to, v_to
        else:
            k_from, v_from = k_in.at[source, k_part], v_in.at[source, v_part]
        return [
            remote(k_from, k_to, w_send.at[route, 0, slot], w_recv.at[route, 0, slot], **where),
            remote(v_from, v_to, w_send.at[route, 1, slot], w_recv.at[route, 1, slot], **where),
        ]

    def far_copies(slot):
        kind, i = SLOTS[slot]
        pair = i if kind == 1 else KEPT + i
        return w_copies(0, slot, kind, i, pl.ds(2 * pair, 2), {"seq": cross if kind == 1 else diagonal})

    def send_weights(pair):
        def across():
            for copy in far_copies(pair):
                copy.start()

        def beside():
            for copy in far_copies(PAIRS + pair - KEPT):
                copy.start()

        on(outer, pair >= KEPT, across)
        if pair >= KEPT:
            pl.when(inner)(beside)

    def weights_sent(pair):
        def across():
            for copy in far_copies(pair):
                copy.wait_send()

        def beside():
            for copy in far_copies(PAIRS + pair - KEPT):
                copy.wait_send()

        on(outer, pair >= KEPT, across)
        if pair >= KEPT:
            pl.when(inner)(beside)

    def plane_copies(route, slot):
        where = ({"rep": 1 - rep}, {"groups": 1 - group}, {"groups": 1 - group})[route - 1]
        kind, i = SLOTS[slot]
        if route < 3:
            return w_copies(route, slot, kind, i, None, where)
        return second_copies(slot, kind, i)

    def second_copies(slot, kind, i):
        piece = 2 * (1 - rep) + group
        k_part = pl.ds(pl.multiple_of(piece * (nope // ROUTES), 16), nope // ROUTES)
        v_part = pl.ds(pl.multiple_of(piece * (width // ROUTES), 16), width // ROUTES)
        both = pl.ds(2 * i, 2)
        return [
            remote(wk.at[kind, both, k_part], wk.at[kind, both, k_part],
                   w_send.at[3, 0, slot], w_recv.at[3, 0, slot], groups=1 - group),
            remote(wv.at[kind, both, v_part], wv.at[kind, both, v_part],
                   w_send.at[3, 1, slot], w_recv.at[3, 1, slot], groups=1 - group),
        ]

    def dq_copy(kind, i):
        owner = jnp.where(kind == 0, me, jnp.where(kind == 1, cross, diagonal))
        return remote(dq_buf.at[kind, pl.ds(2 * i, 2)], dq_out.at[pl.ds(owner * heads + first_head(kind, i), 2)],
                      dq_send.at[kind, i], dq_recv.at[kind, i], seq=near)

    def x_copies(kind, h):
        return [
            remote(kx_out.at[kind, h], kx_in.at[kind, h], kx_sem.at[0, kind, h], kx_sem.at[1, kind, h],
                   rep=1 - rep),
            remote(vx_out.at[kind, h], vx_in.at[kind, h], vx_sem.at[0, kind, h], vx_sem.at[1, kind, h],
                   rep=1 - rep),
        ]

    def z_copies(kind, h):
        where = {"seq": cross if kind == 1 else diagonal}
        at = h if kind == 1 else 2 * KEPT + h
        return [
            remote(kz_out.at[kind - 1, h], kz_in.at[at], kz_send.at[kind - 1, h], kz_recv.at[at], **where),
            remote(vz_out.at[kind - 1, h], vz_in.at[at], vz_send.at[kind - 1, h], vz_recv.at[at], **where),
        ]

    own = pl.ds(me * heads, heads)
    over = pl.ds(cross * heads, heads)
    extra = pl.ds(diagonal * heads + 2 * KEPT, 2 * EXTRA)
    locals_ = [
        pltpu.make_async_copy(lat_in, lat_buf.at[me], own_sem.at[0]),
        pltpu.make_async_copy(q_in.at[own], q_buf.at[0, place], own_sem.at[1]),
        pltpu.make_async_copy(g_in.at[own], g_buf.at[0, place], own_sem.at[2]),
        pltpu.make_async_copy(k_in, wk.at[0], own_sem.at[3]),
        pltpu.make_async_copy(v_in, wv.at[0], own_sem.at[4]),
        pltpu.make_async_copy(q_in.at[over], q_buf.at[1, place], own_sem.at[5]),
        pltpu.make_async_copy(g_in.at[over], g_buf.at[1, place], own_sem.at[6]),
        pltpu.make_async_copy(q_in.at[extra], q_buf.at[2, place, pl.ds(0, 2 * EXTRA)], own_sem.at[7]),
        pltpu.make_async_copy(g_in.at[extra], g_buf.at[2, place, pl.ds(0, 2 * EXTRA)], own_sem.at[8]),
    ]
    for copy in locals_:
        copy.start()

    barrier = pltpu.get_barrier_semaphore()
    others = ({"seq": near}, {"seq": cross}, {"rep": 1 - rep}, {"groups": 1 - group},
              {"seq": diagonal}, {"sub": 1 - sub})
    for where in others:
        pl.semaphore_signal(barrier, inc=1, device_id=where, device_id_type=pl.DeviceIdType.MESH)
    pl.semaphore_wait(barrier, len(others))

    @pl.when(side == 0)
    def _():
        lat_cross.start()

    lat_near.start()
    send_weights(0)

    @pl.when(side == 1)
    def _():
        lat_cross.wait_recv()
        lat_relay.start()
        share_cross.start()

    for at in range(AHEAD):
        send_task(*TASKS[at])
        if at + 1 < PAIRS:
            send_weights(at + 1)

    key_at = lax.broadcasted_iota(jnp.int32, (BLK, BLK), 0)
    query_at = lax.broadcasted_iota(jnp.int32, (BLK, BLK), 1)
    for key_block in range(total // BLK):
        for t in range(2):
            query_block = 2 * side + t
            hit = jnp.int32(0)
            for m in range(slots.shape[0]):
                same = (slots[m, query_block] == key_block) & (m < counts[query_block])
                hit = hit | same.astype(jnp.int32)
            wide = jnp.full((BLK, BLK), hit, jnp.int32) > 0
            wide = wide & (key_at + key_block * BLK <= query_at + query_block * BLK)
            bias[key_block * BLK : (key_block + 1) * BLK, t * BLK : (t + 1) * BLK] = jnp.where(
                wide, 0.0, -1e30).astype(jnp.float32)
    dlat[...] = jnp.zeros_like(dlat)
    for copy in locals_:
        copy.wait()

    def fill(b):
        columns = slice(b * BLK, (b + 1) * BLK)
        lat_t[:, columns] = lat_buf[b]
        lat[columns, :] = lat_buf[b, :width, :].T
        keys[columns, nope:query_width] = lat_buf[b, width:, :].T
        keys_t[nope:, columns] = lat_buf[b, width:, :]

    lat_near.wait()
    share_near.start()

    @pl.when(side == 0)
    def _():
        lat_cross.wait_send()
        share_near.wait()
        for b in range(2):
            fill(b)
        lat_t[:, 2 * BLK:] = jnp.zeros((kv_width, total - 2 * BLK), jnp.bfloat16)
        lat[2 * BLK:, :] = jnp.zeros((total - 2 * BLK, width), jnp.bfloat16)
        keys[2 * BLK:, nope:query_width] = jnp.zeros((total - 2 * BLK, query_width - nope), jnp.bfloat16)
        keys_t[nope:, 2 * BLK:] = jnp.zeros((query_width - nope, total - 2 * BLK), jnp.bfloat16)

    @pl.when(side == 1)
    def _():
        lat_relay.wait()
        share_diagonal.start()
        share_near.wait()
        share_cross.wait()
        share_diagonal.wait()
        for b in range(4):
            fill(b)

    def from_far(slot):
        def act():
            for copy in far_copies(slot):
                copy.wait_recv()
            for copy in plane_copies(1, slot) + plane_copies(2, slot):
                copy.start()
        on(inner, inner_only(*SLOTS[slot]), act)

    def from_side(slot):
        def act():
            for copy in plane_copies(1, slot):
                copy.wait()
            for copy in plane_copies(3, slot):
                copy.start()
        on(inner, inner_only(*SLOTS[slot]), act)

    def from_beside(slot):
        def act():
            for copy in plane_copies(2, slot) + plane_copies(3, slot):
                copy.wait()
        on(inner, inner_only(*SLOTS[slot]), act)

    def sum_slot(slot):
        kind, i = SLOTS[slot]

        def act():
            for h in (2 * i, 2 * i + 1):
                for copy in x_copies(kind, h):
                    copy.wait()
                kz_out[kind - 1, h] = (k_keep[kind, h] + kx_in[kind, h].astype(jnp.float32)).astype(jnp.bfloat16)
                vz_out[kind - 1, h] = (v_keep[kind, h] + vx_in[kind, h].astype(jnp.float32)).astype(jnp.bfloat16)
                for copy in z_copies(kind, h):
                    copy.start()
        on(inner, inner_only(kind, i), act)

    def one_step(n, unused):
        kind = jnp.int32(0)
        i = jnp.int32(0)
        active = jnp.int32(1)
        for at, (its_kind, its_pair) in enumerate(TASKS):
            kind = jnp.where(n == at, its_kind, kind)
            i = jnp.where(n == at, its_pair, i)
            if inner_only(its_kind, its_pair):
                active = jnp.where((n == at) & outer, 0, active)

        for at in range(len(TASKS)):
            @pl.when(n == at)
            def _():
                if at + AHEAD < len(TASKS):
                    send_task(*TASKS[at + AHEAD])
                if 1 <= at <= len(SLOTS):
                    from_side(at - 1)
                if at < len(SLOTS):
                    from_far(at)
                if 2 <= at <= LAST_SLOT:
                    from_beside(at - 2)

        @pl.when(active == 1)
        def _():
            q_copy(kind, i).wait_recv()
            g_copy(kind, i).wait_recv()
            owner = jnp.where(kind == 0, me, jnp.where(kind == 1, cross, diagonal))
            first = owner * heads + first_head(kind, i)

            def one_head(c, unused):
                h = 2 * i + c
                q2 = jnp.concatenate([q_buf[kind, 0, h], q_buf[kind, 1, h]], axis=1)
                g2 = jnp.concatenate([g_buf[kind, 0, h], g_buf[kind, 1, h]], axis=0)
                dq, latent_part, rope, k_grad, v_grad = head_math(
                    q2, g2, wk[kind, h], wv[kind, h], lat_t, lat, bias, keys, keys_t
                )
                dq_out[first + c] = jnp.where(place == 0, dq[:, :BLK], dq[:, BLK:])
                dq_buf[kind, h] = jnp.where(place == 0, dq[:, BLK:], dq[:, :BLK])
                dlat[:width, :] += latent_part
                dlat[width:, :] += rope
                k_half[...] = k_grad
                v_half[...] = v_grad
                kx_out[kind, h] = k_half[pl.ds((1 - rep) * k_rows, k_rows), :].astype(jnp.bfloat16)
                vx_out[kind, h] = v_half[pl.ds((1 - rep) * v_rows, v_rows), :].astype(jnp.bfloat16)

                @pl.when(n > 1)
                def _():
                    for copy in x_copies(kind, h):
                        copy.start()

                k_keep[kind, h] = k_half[pl.ds(rep * k_rows, k_rows), :]
                v_keep[kind, h] = v_half[pl.ds(rep * v_rows, v_rows), :]
                return unused

            lax.fori_loop(0, 2, one_head, 0)
            dq_copy(kind, i).start()

        for at in range(3, len(TASKS)):
            @pl.when(n == at)
            def _():
                if at - 3 < len(SLOTS):
                    sum_slot(at - 3)
                if at == LAST_SLOT:
                    for h in range(4):
                        for copy in x_copies(0, h):
                            copy.start()

        return unused

    lax.fori_loop(0, len(TASKS), one_step, 0)

    exchange = remote(dlat.at[pl.ds((1 - sub) * half_rows, half_rows), :], half_in,
                      half_sem.at[0], half_sem.at[1], sub=1 - sub)
    exchange.start()
    exchange.wait()
    half_in[...] += dlat[pl.ds(sub * half_rows, half_rows), :]

    def columns_of(block):
        return half_in[:, pl.ds(pl.multiple_of(block * BLK, BLK), BLK)]

    def piece(slot):
        return remote(piece_out.at[slot], piece_in.at[slot], piece_send.at[slot], piece_recv.at[slot], seq=near)

    across = remote(cross_out, cross_in, piece_send.at[2], piece_recv.at[2], seq=cross)
    piece_out[0] = columns_of(near).astype(jnp.bfloat16)
    piece(0).start()

    @pl.when(side == 1)
    def _():
        piece_out[1] = columns_of(diagonal).astype(jnp.bfloat16)
        piece(1).start()
        piece(1).wait()
        cross_out[...] = (columns_of(cross) + piece_in[1].astype(jnp.float32)).astype(jnp.bfloat16)
        across.start()

    piece(0).wait()
    lat_out[...] = columns_of(me) + piece_in[0].astype(jnp.float32)

    def finish(h, unused):
        for copy in x_copies(0, h):
            copy.wait()
        remote(kz_out.at[0, h], kz_in.at[h], kz_send.at[0, h], kz_recv.at[h], seq=cross).wait_recv()
        remote(vz_out.at[0, h], vz_in.at[h], vz_send.at[0, h], vz_recv.at[h], seq=cross).wait_recv()
        dk_out[h] = k_keep[0, h] + kx_in[0, h].astype(jnp.float32) + kz_in[h].astype(jnp.float32)
        dv_out[h] = v_keep[0, h] + vx_in[0, h].astype(jnp.float32) + vz_in[h].astype(jnp.float32)
        return unused

    lax.fori_loop(0, heads, finish, 0)

    @pl.when(side == 0)
    def _():
        across.wait_recv()
        lat_out[...] += cross_in[...].astype(jnp.float32)

    @pl.when(side == 1)
    def _():
        across.wait_send()

    for pair in range(PAIRS):
        weights_sent(pair)
    for slot, (kind, i) in enumerate(SLOTS):
        def sums_sent():
            for h in (2 * i, 2 * i + 1):
                for copy in z_copies(kind, h):
                    copy.wait_send()
        on(inner, inner_only(kind, i), sums_sent)
    for kind, i in TASKS:
        def to_near():
            q_copy(kind, i).wait_send()
            g_copy(kind, i).wait_send()
            dq_copy(kind, i).wait_recv()

        def from_here():
            dq_copy(kind, i).wait_send()
        on(outer, inner_only(kind, i), to_near)
        on(inner, inner_only(kind, i), from_here)


def local_small(queries, grad_out, latent_kv, key_up, value_up, key_blocks, block_counts):
    shards = lax.axis_size("seq")
    heads, _, nope, width = key_up.shape
    value_width = value_up.shape[3]
    q_t = jnp.transpose(queries[0], (1, 2, 0))
    g_t = jnp.transpose(grad_out[0], (1, 0, 2))
    lat_local = latent_kv[0].T
    kv_width, tokens = lat_local.shape
    total = shards * tokens
    query_width = q_t.shape[1]
    half = kv_width // 2
    pairs = heads // 2
    bf16, f32 = jnp.bfloat16, jnp.float32
    hbm = pl.BlockSpec(memory_space=pl.ANY)
    vmem = pl.BlockSpec(memory_space=pltpu.VMEM)
    smem = pl.BlockSpec(memory_space=pltpu.SMEM)
    sems = lambda *shape: pltpu.SemaphoreType.DMA(shape)
    k_part, v_part = (nope // 2, width), (width // 2, value_width)
    dq, dlat, dk, dv = pl.pallas_call(
        functools.partial(attention_kernel, heads),
        in_specs=[smem, smem, hbm, hbm, hbm, hbm, hbm],
        out_specs=[vmem, vmem, vmem, vmem],
        out_shape=[
            jax.ShapeDtypeStruct(q_t.shape, bf16),
            jax.ShapeDtypeStruct((half, tokens), f32),
            jax.ShapeDtypeStruct((heads, *k_part), f32),
            jax.ShapeDtypeStruct((heads, *v_part), f32),
        ],
        scratch_shapes=[
            pltpu.VMEM((3, 2, heads, query_width, tokens), bf16),
            pltpu.VMEM((3, 2, heads, tokens, value_width), bf16),
            pltpu.VMEM((shards, kv_width, tokens), bf16),
            pltpu.VMEM((3, heads, nope, width), bf16),
            pltpu.VMEM((3, heads, width, value_width), bf16),
            pltpu.VMEM((3, heads, query_width, tokens), bf16),
            pltpu.VMEM((kv_width, total), bf16),
            pltpu.VMEM((total, width), bf16),
            pltpu.VMEM((total, 2 * BLK), f32),
            pltpu.VMEM((total, 2 * BLK), bf16),
            pltpu.VMEM((query_width, total), bf16),
            pltpu.VMEM((kv_width, total), f32),
            pltpu.VMEM((nope, width), f32),
            pltpu.VMEM((width, value_width), f32),
            pltpu.VMEM((3, heads, *k_part), f32),
            pltpu.VMEM((3, heads, *v_part), f32),
            pltpu.VMEM((3, heads, *k_part), bf16),
            pltpu.VMEM((3, heads, *k_part), bf16),
            pltpu.VMEM((3, heads, *v_part), bf16),
            pltpu.VMEM((3, heads, *v_part), bf16),
            pltpu.VMEM((2, heads, *k_part), bf16),
            pltpu.VMEM((heads, *k_part), bf16),
            pltpu.VMEM((2, heads, *v_part), bf16),
            pltpu.VMEM((heads, *v_part), bf16),
            pltpu.VMEM((half, total), f32),
            pltpu.VMEM((2, half, tokens), bf16),
            pltpu.VMEM((2, half, tokens), bf16),
            pltpu.VMEM((half, tokens), bf16),
            pltpu.VMEM((half, tokens), bf16),
            sems(3, pairs), sems(3, pairs), sems(3, pairs), sems(3, pairs),
            sems(3), sems(3), sems(3), sems(3),
            sems(ROUTES, 2, len(SLOTS)), sems(ROUTES, 2, len(SLOTS)),
            sems(3, pairs), sems(3, pairs),
            sems(2, 3, heads), sems(2, 3, heads), sems(2, heads), sems(heads), sems(2, heads), sems(heads),
            sems(2), sems(3), sems(3), sems(9),
        ],
        compiler_params=pltpu.CompilerParams(
            collective_id=0, has_side_effects=True, vmem_limit_bytes=40 << 20
        ),
    )(key_blocks[0].T, block_counts[0], q_t, g_t, lat_local, key_up[:, 0], value_up[:, 0])
    return (
        jnp.transpose(dq, (2, 0, 1))[None],
        dlat.T[None],
        dk[:, None],
        dv[:, None],
    )


def head_backward(
    head_queries, head_grads, latent, key_weight, value_weight, slot_list, count_list, block_rows
):
    length = head_queries.shape[0]
    latent_width = key_weight.shape[1]
    nope_width = key_weight.shape[0]
    query_width = head_queries.shape[1]
    value_width = head_grads.shape[1]
    block_count = length // block_rows
    slot_count = slot_list.shape[1]
    factor = 1.0 / math.sqrt(query_width)
    compressed = latent[:, :latent_width]
    key_nope = jnp.einsum(
        "tl,dl->td", compressed, key_weight, preferred_element_type=jnp.float32
    ).astype(jnp.bfloat16)
    values = jnp.dot(compressed, value_weight, preferred_element_type=jnp.float32).astype(
        jnp.bfloat16
    )
    keys_all = jnp.concatenate([key_nope, latent[:, latent_width:]], axis=1)
    per_group = math.gcd(block_count, max(1, 512 // block_rows))
    group_count = block_count // per_group
    key_tiles = keys_all.reshape(block_count, block_rows, query_width)
    value_tiles = values.reshape(block_count, block_rows, value_width)
    causal = lax.broadcasted_iota(jnp.int32, (block_rows, block_rows), 0) >= lax.broadcasted_iota(
        jnp.int32, (block_rows, block_rows), 1
    )
    slot_range = jnp.arange(slot_count, dtype=jnp.int32)
    within = jnp.arange(per_group, dtype=jnp.int32)

    def tiles_at(tiles, group_slots):
        return jnp.stack([
            jnp.concatenate([
                lax.dynamic_index_in_dim(tiles, group_slots[b, m], 0, keepdims=False)
                for m in range(slot_count)
            ])
            for b in range(per_group)
        ])

    def one_group(carry, inputs):
        key_total, value_total = carry
        query_tile, grad_tile, group_slots, group_counts, group_index = inputs
        own_blocks = group_index * per_group + within
        keys_here = tiles_at(key_tiles, group_slots)
        values_here = tiles_at(value_tiles, group_slots)
        live = slot_range[None, :] < group_counts[:, None]
        diagonal = group_slots == own_blocks[:, None]
        allowed = live[:, None, :, None] & (
            jnp.logical_not(diagonal)[:, None, :, None] | causal[None, :, None, :]
        )
        allowed = allowed.reshape(per_group, block_rows, slot_count * block_rows)
        scores = (
            jnp.einsum("gqd,gkd->gqk", query_tile, keys_here, preferred_element_type=jnp.float32)
            * factor
        )
        scores = jnp.where(allowed, scores, -1e30)
        top_score = jnp.max(scores, axis=2, keepdims=True)
        expo = jnp.where(allowed, jnp.exp(scores - top_score), 0.0)
        probs = expo / jnp.sum(expo, axis=2, keepdims=True)
        probs_b = probs.astype(jnp.bfloat16)
        attended = jnp.einsum(
            "gqk,gkd->gqd", probs_b, values_here, preferred_element_type=jnp.float32
        )
        delta = jnp.sum(grad_tile.astype(jnp.float32) * attended, axis=2, keepdims=True)
        grad_probs = jnp.einsum(
            "gqd,gkd->gqk", grad_tile, values_here, preferred_element_type=jnp.float32
        )
        grad_scores = (probs * (grad_probs - delta)).astype(jnp.bfloat16)
        grad_query = (
            jnp.einsum("gqk,gkd->gqd", grad_scores, keys_here, preferred_element_type=jnp.float32)
            * factor
        ).astype(jnp.bfloat16)
        grad_key = (
            jnp.einsum("gqk,gqd->gkd", grad_scores, query_tile, preferred_element_type=jnp.float32)
            * factor
        )
        grad_value = jnp.einsum(
            "gqk,gqd->gkd", probs_b, grad_tile, preferred_element_type=jnp.float32
        )
        flat_slots = group_slots.reshape(per_group * slot_count)
        key_total = key_total.at[flat_slots].add(
            grad_key.reshape(per_group * slot_count, block_rows, query_width)
        )
        value_total = value_total.at[flat_slots].add(
            grad_value.reshape(per_group * slot_count, block_rows, value_width)
        )
        return ((key_total, value_total), grad_query)

    start = (
        jnp.zeros((block_count, block_rows, query_width), jnp.float32),
        jnp.zeros((block_count, block_rows, value_width), jnp.float32),
    )
    inputs = (
        head_queries.reshape(group_count, per_group, block_rows, query_width),
        head_grads.reshape(group_count, per_group, block_rows, value_width),
        slot_list.reshape(group_count, per_group, slot_count),
        count_list.reshape(group_count, per_group),
        jnp.arange(group_count, dtype=jnp.int32),
    )
    (key_total, value_total), grad_tiles = lax.scan(one_group, start, inputs)
    grad_query = grad_tiles.reshape(length, query_width)
    key_grads = key_total.reshape(length, query_width)
    nope_grads = key_grads[:, :nope_width].astype(jnp.bfloat16)
    value_grads = value_total.reshape(length, value_width).astype(jnp.bfloat16)
    latent_grad = jnp.dot(nope_grads, key_weight, preferred_element_type=jnp.float32) + jnp.einsum(
        "tv,lv->tl", value_grads, value_weight, preferred_element_type=jnp.float32
    )
    head_part = jnp.concatenate([latent_grad, key_grads[:, nope_width:]], axis=1).astype(
        jnp.bfloat16
    )
    key_weight_grad = jnp.einsum(
        "td,tl->dl", nope_grads, compressed, preferred_element_type=jnp.float32
    )
    value_weight_grad = jnp.einsum(
        "tl,tv->lv", compressed, value_grads, preferred_element_type=jnp.float32
    )
    return (grad_query, head_part, key_weight_grad, value_weight_grad)


def local_general(queries, grad_out, latent_kv, key_up, value_up, key_blocks, block_counts):
    head_queries, head_grads = (
        lax.all_to_all(queries, "seq", split_axis=2, concat_axis=1, tiled=True),
        lax.all_to_all(grad_out, "seq", split_axis=2, concat_axis=1, tiled=True),
    )
    latent = lax.all_gather(latent_kv, "seq", axis=1, tiled=True)[0]
    slot_list = key_blocks[0]
    count_list = block_counts[0]
    query_stack = jnp.moveaxis(head_queries[0], 1, 0)
    grad_stack = jnp.moveaxis(head_grads[0], 1, 0)

    def one_head(carry, inputs):
        head_q, head_g, key_weight, value_weight = inputs
        results = head_backward(
            head_q, head_g, latent, key_weight, value_weight, slot_list, count_list, BLK
        )
        return (carry, results)

    unused, (query_grads, head_parts, key_grads, value_grads) = lax.scan(
        one_head,
        jnp.zeros((), jnp.float32),
        (query_stack, grad_stack, key_up[:, 0], value_up[:, 0]),
    )
    returning = jnp.moveaxis(query_grads, 0, 1)[None]
    grad_queries = lax.all_to_all(returning, "seq", split_axis=1, concat_axis=2, tiled=True)
    heads_here, length, part_width = head_parts.shape
    seq_count = lax.axis_size("seq")
    tokens_here = length // seq_count
    pieces = head_parts.reshape(heads_here, seq_count, tokens_here, part_width)
    arrived = lax.all_to_all(pieces, "seq", split_axis=1, concat_axis=1, tiled=True)
    summed = jnp.sum(arrived.astype(jnp.float32), axis=(0, 1))
    grad_latent = lax.psum_scatter(summed, "sub", scatter_dimension=1, tiled=True)
    key_grads = key_grads[:, None]
    value_grads = value_grads[:, None]
    total_key, total_value = lax.psum((key_grads, value_grads), "rep")
    replica_count = lax.axis_size("rep")
    replica_index = lax.axis_index("rep")
    key_rows = total_key.shape[2] // replica_count
    value_rows = total_value.shape[2] // replica_count
    grad_key_up = lax.dynamic_slice_in_dim(total_key, replica_index * key_rows, key_rows, 2)
    grad_value_up = lax.dynamic_slice_in_dim(total_value, replica_index * value_rows, value_rows, 2)
    return (grad_queries, grad_latent[None], grad_key_up, grad_value_up)


def solution(mesh):
    placed = (
        P(("groups", "rep"), "seq", None, "sub"),
        P(("groups", "rep"), "seq", None, "sub"),
        P(("groups", "rep"), "seq", None),
        P("seq", "sub", None, None),
        P("seq", "sub", None, None),
        P(("groups", "rep"), None, None),
        P(("groups", "rep"), None),
    )

    def local(queries, grad_out, latent_kv, key_up, value_up, key_blocks, block_counts):
        args = (queries, grad_out, latent_kv, key_up, value_up, key_blocks, block_counts)
        shards = mesh.shape["seq"]
        small = (
            queries.shape[1] == BLK
            and shards == 4
            and mesh.shape["rep"] == 2
            and mesh.shape["sub"] == 2
            and mesh.shape["groups"] == 2
            and key_up.shape[0] == 2 * PAIRS
            and latent_kv.shape[2] % 32 == 0
        )
        return local_small(*args) if small else local_general(*args)

    return jax.shard_map(
        local,
        mesh=mesh,
        in_specs=placed,
        out_specs=(
            P(("groups", "rep"), "seq", None, "sub"),
            P(("groups", "rep"), "seq", "sub"),
            P(("groups", "seq"), "sub", "rep", None),
            P(("groups", "seq"), "sub", "rep", None),
        ),
        check_vma=False,
    )
```
